32 devices in a mesh: ctx: 16 (over z, y, core), tp: 2 (over x).
Axes of the slice: x: 2, y: 2, z: 4, core: 2. Of those that a mesh axis runs over, the one named last changes fastest.
Arguments:
- queries: bfloat16 [1024, 1536], P('ctx', 'tp'), may hold values from -512 to 512
- keys: bfloat16 [1024, 1536], P('ctx', 'tp'), may hold values from -8 to 8
- values: bfloat16 [1024, 1536], P('ctx', 'tp'), may hold values from -6 to 6
- wo: bfloat16 [1536, 3072], P('tp'), may hold values from -0.15625 to 0.15625
- frame_tokens: int32 [16], replicated, may hold values from 32 to 64, as said below
Outputs:
- projected: bfloat16 [1024, 3072], P(('ctx', 'tp'))
The draws below stay inside these ranges and needn't reach their ends.
Inputs may be any that keep to these rules, and one draw needn't show every extreme that they name: `frame_tokens`: at least 32 tokens of every frame are live.
All inputs are finite; a program needn't handle non-finite values.
Results may differ from the reference program's by a relative error of at most 0.014.
Values may be sent and summed in bfloat16 or wider, within the bound.
A program may use at most 128 MiB of HBM per device.

```python
import math
import jax
import jax.numpy as jnp
from jax import lax

WIDTH = 3072
HEADS = 12
HEAD_DIM = 128
FRAME = 64
FRAMES = 16
TOKENS = 1024


def shared_fields(key):
    columns = HEADS * HEAD_DIM
    key_drawn = jnp.clip(jax.random.normal(jax.random.fold_in(key, 11), (TOKENS, columns), jnp.float32), -6.0, 6.0)
    query_drawn = jnp.clip(2.5 * jax.random.normal(jax.random.fold_in(key, 12), (TOKENS, columns), jnp.float32), -15.0, 15.0)
    return (key_drawn, query_drawn)


def draw_queries(key, part):
    key_field, query_field = shared_fields(key)
    return query_field.astype(jnp.bfloat16)


def draw_keys(key, part):
    key_field, query_field = shared_fields(key)
    return key_field.astype(jnp.bfloat16)


def draw_frame_tokens(key, part):
    counts = jax.random.randint(jax.random.fold_in(key, 21), (FRAMES,), FRAME // 2, FRAME + 1)
    fullest = jax.random.randint(jax.random.fold_in(key, 22), (), 0, FRAMES)
    emptiest = jax.random.randint(jax.random.fold_in(key, 23), (), 0, FRAMES)
    frame_ids = jnp.arange(FRAMES, dtype=jnp.int32)
    counts = jnp.where(frame_ids == emptiest, FRAME // 2, counts)
    counts = jnp.where(frame_ids == fullest, FRAME, counts)
    return counts.astype(jnp.int32)


def shard_levels(own_key, dims, cuts, smallest, high):
    level, own = 1.0, jax.random.fold_in(own_key, 6)
    for dim, shards_of in cuts:
        steps = jnp.exp(jax.random.uniform(jax.random.fold_in(own, dim), (shards_of,), jnp.float32, smallest / len(cuts), high / len(cuts)))
        level = level * jnp.repeat(steps, dims[dim] // shards_of).reshape([-1 if axis == dim else 1 for axis in range(len(dims))])
    return level


def normal_values(rng, extent, deviation, bound, cuts=(), kind=jnp.bfloat16):
    gain = shard_levels(rng, extent, cuts, -0.22, 0.18) if cuts else 1.0
    values = jax.random.normal(rng, extent, jnp.float32) * deviation * gain
    return jnp.minimum(jnp.maximum(values, -bound), bound).astype(kind)


def setup_inputs(seed: int = 0) -> dict:
    arg_keys = jax.random.split(jax.random.key(seed), 6)
    queries = draw_queries(jax.random.fold_in(arg_keys[5], 71), 0)
    keys = draw_keys(jax.random.fold_in(arg_keys[5], 71), 0)
    values = normal_values(arg_keys[2], (TOKENS, HEADS * HEAD_DIM), 1.0, 6.0, ((0, 16), (1, 2)))
    wo = normal_values(arg_keys[3], (HEADS * HEAD_DIM, WIDTH), (HEADS * HEAD_DIM) ** -0.5, 0.15625, ((0, 2),))
    frame_tokens = draw_frame_tokens(jax.random.fold_in(arg_keys[5], 71), 0)
    return {"queries": queries, "keys": keys, "values": values, "wo": wo, "frame_tokens": frame_tokens}


def reference(queries, keys, values, wo, frame_tokens):
    total_rows = queries.shape[0]
    positions = jnp.arange(total_rows, dtype=jnp.int32)
    frame_index = positions // FRAME
    live_mask = positions % FRAME < frame_tokens[frame_index]
    query_all = queries.astype(jnp.float32).reshape(total_rows, HEADS, HEAD_DIM)
    key_all = keys.astype(jnp.float32).reshape(total_rows, HEADS, HEAD_DIM)
    value_all = values.astype(jnp.float32).reshape(total_rows, HEADS, HEAD_DIM)
    block_rows = 512 if total_rows % 512 == 0 else total_rows
    scale_factor = 1.0 / math.sqrt(HEAD_DIM)

    def one_block(start):
        query_block = lax.dynamic_slice_in_dim(query_all, start, block_rows, 0)
        frame_block = lax.dynamic_slice_in_dim(frame_index, start, block_rows, 0)
        live_block = lax.dynamic_slice_in_dim(live_mask, start, block_rows, 0)
        scores = jnp.einsum('qhd,khd->hqk', query_block, key_all) * scale_factor
        allowed = (frame_index[None, :] <= frame_block[:, None]) & live_mask[None, :]
        scores = jnp.where(allowed[None], scores, -jnp.inf)
        row_max = lax.optimization_barrier(jnp.max(scores, axis=-1, keepdims=True))
        weights = jnp.exp(scores - row_max)
        totals = lax.optimization_barrier(jnp.sum(weights, axis=-1))
        rounded = lax.optimization_barrier(weights.astype(jnp.bfloat16)).astype(jnp.float32)
        summed = jnp.einsum('hqk,khd->qhd', rounded, value_all)
        heads_out = summed / jnp.transpose(totals)[:, :, None]
        heads_out = jnp.where(live_block[:, None, None], heads_out, 0.0)
        return heads_out.astype(jnp.bfloat16)
    block_starts = jnp.arange(0, total_rows, block_rows, dtype=jnp.int32)
    blocks_out = lax.map(one_block, block_starts)
    attended = blocks_out.reshape(total_rows, HEADS * HEAD_DIM)
    return jnp.dot(attended, wo, preferred_element_type=jnp.float32).astype(jnp.bfloat16)
```

```python
import functools
import math

import jax
import jax.numpy as jnp
from jax import lax
from jax.experimental import pallas as pl
from jax.experimental.pallas import tpu as pltpu
from jax.sharding import PartitionSpec as P

HEAD_DIM = 128
LAYER = 4
NEG = -1e30
MESH = pl.DeviceIdType.MESH
UP, SIDE, CORE, CROSS = 0, 1, 2, 3


def kernel(
    n,
    chunk,
    counts_ref,
    q_ref,
    k_hbm,
    v_hbm,
    wo_hbm,
    out_ref,
    k_all,
    v_all,
    wo_all,
    run_max,
    run_total,
    run_acc,
    attended,
    kept,
    outgoing,
    incoming,
    send_sem,
    recv_sem,
    local_sem,
    wo_sem,
    x_send_sem,
    x_recv_sem,
):
    tok_rows, columns = q_ref.shape
    head_count = columns // HEAD_DIM
    width = wo_hbm.shape[1]
    half = tok_rows // 2
    me = lax.axis_index("ctx")
    tp = lax.axis_index("tp")
    levels = n // LAYER
    level = me // LAYER
    lane = lax.rem(me, LAYER)
    base = level * LAYER
    side_y = lax.rem(lane + 2, LAYER)
    core_lane = lane + 1 - 2 * lax.rem(lane, 2)
    cross_lane = lax.rem(core_lane + 2, LAYER)
    above = lax.rem(me + LAYER, n)
    below = lax.rem(me + n - LAYER, n)
    has_above = level < levels - 1
    has_below = level > 0
    side_dev, core_dev = base + side_y, base + core_lane
    halls = (k_all, v_all)
    inputs = (k_hbm, v_hbm)

    wo_copy = pltpu.make_async_copy(wo_hbm, wo_all, wo_sem)
    wo_copy.start()

    def rows_of(src):
        return pl.ds(pl.multiple_of(src * tok_rows, tok_rows), tok_rows)

    own = [
        pltpu.make_async_copy(inputs[p], halls[p].at[rows_of(me)], local_sem.at[p])
        for p in range(2)
    ]
    for p in range(2):
        own[p].start()

    barrier = pltpu.get_barrier_semaphore()

    def greet(dev, other_tp):
        pl.semaphore_signal(barrier, inc=1, device_id=(dev, other_tp), device_id_type=MESH)

    @pl.when(has_above)
    def _():
        greet(above, tp)

    @pl.when(has_below)
    def _():
        greet(below, tp)

    greet(side_dev, tp)
    greet(core_dev, tp)
    greet(me, 1 - tp)
    pl.semaphore_wait(
        barrier, 3 + has_above.astype(jnp.int32) + has_below.astype(jnp.int32)
    )

    def piece(p, kind, step, src, dev):
        return pltpu.make_async_remote_copy(
            src_ref=halls[p].at[rows_of(src)],
            dst_ref=halls[p].at[rows_of(src)],
            send_sem=send_sem.at[kind, p, step],
            recv_sem=recv_sem.at[p, src],
            device_id=(dev, tp),
            device_id_type=MESH,
        )

    def forward_chain(step):
        src = me - LAYER * step
        for p in range(2):

            @pl.when(step > 0)
            def _():
                piece(p, UP, step, src, above).wait_recv()

            @pl.when(step == 0)
            def _():
                own[p].wait()

            @pl.when(has_above)
            def _():
                piece(p, UP, step, src, above).start()

            piece(p, SIDE, step, src, side_dev).start()
            piece(p, CORE, step, src, core_dev).start()

    def forward_side(step):
        src = base + side_y - LAYER * step
        for p in range(2):
            piece(p, CROSS, step, src, core_dev).wait_recv()
            piece(p, CROSS, step, src, core_dev).start()

    def wait_core(step):
        for p in range(2):
            for other in (core_lane, cross_lane):
                piece(p, CORE, step, base + other - LAYER * step, core_dev).wait_recv()

    span = LAYER * tok_rows
    col = lax.broadcasted_iota(jnp.int32, (tok_rows, span), 1)
    slot = col // tok_rows
    place = lax.rem(col, tok_rows)
    scale = 1.0 / math.sqrt(HEAD_DIM)

    def attend(step):
        first = base - LAYER * step
        limit = jnp.zeros((tok_rows, span), jnp.int32)
        for f in range(LAYER):
            live = jnp.where(first + f <= me, counts_ref[first + f], 0)
            limit = jnp.where(slot == f, live, limit)
        allowed = place < limit
        keys_at = pl.ds(pl.multiple_of(first * tok_rows, span), span)
        for h in range(head_count):
            cols = slice(h * HEAD_DIM, (h + 1) * HEAD_DIM)
            scores = lax.dot_general(
                q_ref[:, cols],
                k_all[keys_at, cols],
                (((1,), (1,)), ((), ())),
                preferred_element_type=jnp.float32,
            )
            scores = jnp.where(allowed, scores * scale, NEG)
            old_max = run_max[h][:, :1]
            new_max = jnp.maximum(old_max, jnp.max(scores, axis=-1, keepdims=True))
            fade = jnp.exp(old_max - new_max)
            weights = jnp.exp(scores - new_max)
            total = fade * run_total[h][:, :1] + jnp.sum(weights, axis=-1, keepdims=True)
            run_max[h] = jnp.broadcast_to(new_max, (tok_rows, HEAD_DIM))
            run_total[h] = jnp.broadcast_to(total, (tok_rows, HEAD_DIM))
            run_acc[:, cols] = fade * run_acc[:, cols] + jnp.dot(
                weights.astype(jnp.bfloat16),
                v_all[keys_at, cols],
                preferred_element_type=jnp.float32,
            )

    run_max[...] = jnp.full(run_max.shape, NEG, jnp.float32)
    run_total[...] = jnp.zeros(run_total.shape, jnp.float32)
    run_acc[...] = jnp.zeros(run_acc.shape, jnp.float32)

    forward_chain(0)
    forward_side(0)

    def body(step, carry):
        forward_chain(step)
        wait_core(step - 1)
        attend(step - 1)
        forward_side(step)
        return carry

    lax.fori_loop(1, level + 1, body, 0)
    wait_core(level)
    attend(level)

    row = lax.broadcasted_iota(jnp.int32, (tok_rows, HEAD_DIM), 0)
    row_live = row < counts_ref[me]
    for h in range(head_count):
        cols = slice(h * HEAD_DIM, (h + 1) * HEAD_DIM)
        out = jnp.where(row_live, run_acc[:, cols] / run_total[h], 0.0)
        attended[:, cols] = out.astype(jnp.bfloat16)

    wo_copy.wait()
    theirs = attended[pl.ds(pl.multiple_of((1 - tp) * half, half), half), :]
    mine = attended[pl.ds(pl.multiple_of(tp * half, half), half), :]
    lhs = jnp.concatenate([theirs, mine], axis=0)

    def swap(c):
        return pltpu.make_async_remote_copy(
            src_ref=outgoing.at[c],
            dst_ref=incoming.at[c],
            send_sem=x_send_sem.at[c],
            recv_sem=x_recv_sem.at[c],
            device_id=(me, 1 - tp),
            device_id_type=MESH,
        )

    for c in range(width // chunk):
        part = jnp.dot(
            lhs, wo_all[:, c * chunk : (c + 1) * chunk], preferred_element_type=jnp.float32
        )
        outgoing[c] = part[:half].astype(jnp.bfloat16)
        swap(c).start()
        kept[c] = part[half:]

    def drain(step, carry):
        for p in range(2):

            @pl.when(has_above)
            def _():
                piece(p, UP, step, me - LAYER * step, above).wait_send()

            piece(p, SIDE, step, me - LAYER * step, side_dev).wait_send()
            piece(p, CORE, step, me - LAYER * step, core_dev).wait_send()
            piece(p, CROSS, step, me - LAYER * step, core_dev).wait_send()
        return carry

    lax.fori_loop(0, level + 1, drain, 0)
    for c in range(width // chunk):
        swap(c).wait_recv()
        out_ref[:, c * chunk : (c + 1) * chunk] = (
            kept[c] + incoming[c].astype(jnp.float32)
        ).astype(out_ref.dtype)
    for c in range(width // chunk):
        swap(c).wait_send()


def on_device(queries, keys, values, wo, frame_tokens):
    tok_rows, columns = queries.shape
    width = wo.shape[1]
    n = lax.axis_size("ctx")
    half = tok_rows // 2
    chunk = 512 if width % 512 == 0 else width
    chunks = width // chunk
    head_count = columns // HEAD_DIM
    levels = n // LAYER
    vmem = pltpu.VMEM
    dma = pltpu.SemaphoreType.DMA
    return pl.pallas_call(
        functools.partial(kernel, n, chunk),
        out_shape=jax.ShapeDtypeStruct((half, width), jnp.bfloat16),
        in_specs=[
            pl.BlockSpec(memory_space=pltpu.SMEM),
            pl.BlockSpec(memory_space=vmem),
            pl.BlockSpec(memory_space=pl.ANY),
            pl.BlockSpec(memory_space=pl.ANY),
            pl.BlockSpec(memory_space=pl.ANY),
        ],
        out_specs=pl.BlockSpec(memory_space=vmem),
        scratch_shapes=[
            vmem((n * tok_rows, columns), jnp.bfloat16),
            vmem((n * tok_rows, columns), jnp.bfloat16),
            vmem(wo.shape, jnp.bfloat16),
            vmem((head_count, tok_rows, HEAD_DIM), jnp.float32),
            vmem((head_count, tok_rows, HEAD_DIM), jnp.float32),
            vmem((tok_rows, columns), jnp.float32),
            vmem((tok_rows, columns), jnp.bfloat16),
            vmem((chunks, half, chunk), jnp.float32),
            vmem((chunks, half, chunk), jnp.bfloat16),
            vmem((chunks, half, chunk), jnp.bfloat16),
            dma((4, 2, levels)),
            dma((2, n)),
            dma((2,)),
            dma,
            dma((chunks,)),
            dma((chunks,)),
        ],
        compiler_params=pltpu.CompilerParams(
            collective_id=0, has_side_effects=True, vmem_limit_bytes=52 << 20
        ),
    )(frame_tokens, queries, keys, values, wo)


def solution(mesh):
    in_specs = (P("ctx", "tp"), P("ctx", "tp"), P("ctx", "tp"), P("tp", None), P())
    out_specs = P(("ctx", "tp"), None)
    return jax.shard_map(
        on_device, mesh=mesh, in_specs=in_specs, out_specs=out_specs, check_vma=False
    )
```

```python
import functools
import math

import jax
import jax.numpy as jnp
from jax import lax
from jax.experimental import pallas as pl
from jax.experimental.pallas import tpu as pltpu
from jax.sharding import PartitionSpec as P

HEAD_DIM = 128
LAYER = 4
NEG = -1e30
MESH = pl.DeviceIdType.MESH
UP, SIDE, CORE, CROSS = 0, 1, 2, 3


def group_levels(levels):
    return levels // 2 if levels % 2 == 0 else levels


def kernel(
    n,
    chunk,
    counts_ref,
    q_ref,
    k_hbm,
    v_hbm,
    wo_hbm,
    out_ref,
    k_all,
    v_all,
    wo_all,
    run_max,
    run_total,
    run_acc,
    guest_q,
    guest_acc,
    guest_stats,
    far_acc,
    far_stats,
    attended,
    kept,
    outgoing,
    incoming,
    send_sem,
    recv_sem,
    local_sem,
    wo_sem,
    x_send_sem,
    x_recv_sem,
    q_send_sem,
    q_recv_sem,
    back_send_sem,
    back_recv_sem,
):
    tok_rows, columns = q_ref.shape
    head_count = columns // HEAD_DIM
    width = wo_hbm.shape[1]
    half = tok_rows // 2
    me = lax.axis_index("ctx")
    tp = lax.axis_index("tp")
    levels = n // LAYER
    group = group_levels(levels)
    guests = levels - group
    level = me // LAYER
    is_upper = level >= group
    local = lax.rem(level, group)
    is_host = level == (group - 1 if guests else levels)
    lane = lax.rem(me, LAYER)
    base = level * LAYER
    side_y = lax.rem(lane + 2, LAYER)
    core_lane = lane + 1 - 2 * lax.rem(lane, 2)
    cross_lane = lax.rem(core_lane + 2, LAYER)
    above = lax.rem(me + LAYER, n)
    below = lax.rem(me + n - LAYER, n)
    has_above = local < group - 1
    has_below = local > 0
    host = (group - 1) * LAYER + lane
    guest_slot = lax.rem(level, group)
    side_dev, core_dev = base + side_y, base + core_lane
    halls = (k_all, v_all)
    inputs = (k_hbm, v_hbm)

    wo_copy = pltpu.make_async_copy(wo_hbm, wo_all, wo_sem)
    wo_copy.start()

    def rows_of(src):
        return pl.ds(pl.multiple_of(src * tok_rows, tok_rows), tok_rows)

    own = [
        pltpu.make_async_copy(inputs[p], halls[p].at[rows_of(me)], local_sem.at[p])
        for p in range(2)
    ]
    for p in range(2):
        own[p].start()

    barrier = pltpu.get_barrier_semaphore()

    def greet(dev, other_tp):
        pl.semaphore_signal(barrier, inc=1, device_id=(dev, other_tp), device_id_type=MESH)

    @pl.when(has_above)
    def _():
        greet(above, tp)

    @pl.when(has_below)
    def _():
        greet(below, tp)

    greet(side_dev, tp)
    greet(core_dev, tp)
    greet(me, 1 - tp)

    @pl.when(is_upper)
    def _():
        greet(host, tp)

    @pl.when(is_host)
    def _():
        def greet_guest(j, carry):
            greet(me + LAYER * (1 + j), tp)
            return carry

        lax.fori_loop(0, guests, greet_guest, 0)

    pl.semaphore_wait(
        barrier,
        3
        + has_above.astype(jnp.int32)
        + has_below.astype(jnp.int32)
        + is_upper.astype(jnp.int32)
        + guests * is_host.astype(jnp.int32),
    )

    def ask(j):
        return pltpu.make_async_remote_copy(
            src_ref=q_ref,
            dst_ref=guest_q.at[j],
            send_sem=q_send_sem,
            recv_sem=q_recv_sem.at[j],
            device_id=(host, tp),
            device_id_type=MESH,
        )

    def answer(j, p):
        source, target = ((guest_acc.at[j], far_acc), (guest_stats.at[j], far_stats))[p]
        return pltpu.make_async_remote_copy(
            src_ref=source,
            dst_ref=target,
            send_sem=back_send_sem.at[p, j],
            recv_sem=back_recv_sem.at[p],
            device_id=(lax.rem(me + LAYER * (1 + j), n), tp),
            device_id_type=MESH,
        )

    if guests:

        @pl.when(is_upper)
        def _():
            ask(guest_slot).start()

    def piece(p, kind, step, src, dev):
        return pltpu.make_async_remote_copy(
            src_ref=halls[p].at[rows_of(src)],
            dst_ref=halls[p].at[rows_of(src)],
            send_sem=send_sem.at[kind, p, step],
            recv_sem=recv_sem.at[p, src],
            device_id=(dev, tp),
            device_id_type=MESH,
        )

    def forward_chain(step):
        src = me - LAYER * step
        for p in range(2):

            @pl.when(step > 0)
            def _():
                piece(p, UP, step, src, above).wait_recv()

            @pl.when(step == 0)
            def _():
                own[p].wait()

            @pl.when(has_above)
            def _():
                piece(p, UP, step, src, above).start()

            piece(p, SIDE, step, src, side_dev).start()
            piece(p, CORE, step, src, core_dev).start()

    def forward_side(step):
        src = base + side_y - LAYER * step
        for p in range(2):
            piece(p, CROSS, step, src, core_dev).wait_recv()
            piece(p, CROSS, step, src, core_dev).start()

    def wait_core(step):
        for p in range(2):
            for other in (core_lane, cross_lane):
                piece(p, CORE, step, base + other - LAYER * step, core_dev).wait_recv()

    span = LAYER * tok_rows
    col = lax.broadcasted_iota(jnp.int32, (tok_rows, span), 1)
    slot = col // tok_rows
    place = lax.rem(col, tok_rows)
    scale = 1.0 / math.sqrt(HEAD_DIM)

    def attend(step, state, load_query, causal):
        first = base - LAYER * step
        limit = jnp.zeros((tok_rows, span), jnp.int32)
        for f in range(LAYER):
            live = counts_ref[first + f]
            if causal:
                live = jnp.where(first + f <= me, live, 0)
            limit = jnp.where(slot == f, live, limit)
        allowed = place < limit
        keys_at = pl.ds(pl.multiple_of(first * tok_rows, span), span)
        for h in range(head_count):
            cols = slice(h * HEAD_DIM, (h + 1) * HEAD_DIM)
            scores = lax.dot_general(
                load_query(cols),
                k_all[keys_at, cols],
                (((1,), (1,)), ((), ())),
                preferred_element_type=jnp.float32,
            )
            scores = jnp.where(allowed, scores * scale, NEG)
            old_max = run_max[state, h][:, :1]
            new_max = jnp.maximum(old_max, jnp.max(scores, axis=-1, keepdims=True))
            fade = jnp.exp(old_max - new_max)
            weights = jnp.exp(scores - new_max)
            total = fade * run_total[state, h][:, :1] + jnp.sum(weights, axis=-1, keepdims=True)
            run_max[state, h] = jnp.broadcast_to(new_max, (tok_rows, HEAD_DIM))
            run_total[state, h] = jnp.broadcast_to(total, (tok_rows, HEAD_DIM))
            run_acc[state, :, cols] = fade * run_acc[state, :, cols] + jnp.dot(
                weights.astype(jnp.bfloat16),
                v_all[keys_at, cols],
                preferred_element_type=jnp.float32,
            )

    def attend_own(step):
        attend(step, 0, lambda cols: q_ref[:, cols], True)

    spot = lax.broadcasted_iota(jnp.int32, (tok_rows, HEAD_DIM), 1)

    def attend_guests(step, last):
        if not guests:
            return

        @pl.when(is_host)
        def _():
            def one(i, carry):
                j = guests - 1 - i

                @pl.when(step == 0)
                def _():
                    ask(j).wait_recv()

                attend(step, 1 + j, lambda cols: guest_q[j, :, cols], False)
                if last:
                    stats = jnp.zeros((tok_rows, HEAD_DIM), jnp.float32)
                    for h in range(head_count):
                        stats = jnp.where(spot == h, run_max[1 + j, h], stats)
                        stats = jnp.where(spot == head_count + h, run_total[1 + j, h], stats)
                    guest_stats[j] = stats
                    guest_acc[j] = run_acc[1 + j].astype(jnp.bfloat16)
                    answer(j, 1).start()
                    answer(j, 0).start()
                return carry

            lax.fori_loop(0, guests, one, 0)

    run_max[...] = jnp.full(run_max.shape, NEG, jnp.float32)
    run_total[...] = jnp.zeros(run_total.shape, jnp.float32)
    run_acc[...] = jnp.zeros(run_acc.shape, jnp.float32)

    forward_chain(0)
    forward_side(0)

    def body(step, carry):
        forward_chain(step)
        wait_core(step - 1)
        attend_own(step - 1)
        forward_side(step)
        attend_guests(step - 1, False)
        return carry

    lax.fori_loop(1, local + 1, body, 0)
    wait_core(local)
    attend_guests(local, True)
    attend_own(local)

    if guests:

        @pl.when(is_upper)
        def _():
            answer(0, 1).wait_recv()
            answer(0, 0).wait_recv()
            for h in range(head_count):
                cols = slice(h * HEAD_DIM, (h + 1) * HEAD_DIM)
                far_max = far_stats[:, h : h + 1]
                far_total = far_stats[:, head_count + h : head_count + h + 1]
                old_max = run_max[0, h][:, :1]
                new_max = jnp.maximum(old_max, far_max)
                fade, far_fade = jnp.exp(old_max - new_max), jnp.exp(far_max - new_max)
                total = fade * run_total[0, h][:, :1] + far_fade * far_total
                run_total[0, h] = jnp.broadcast_to(total, (tok_rows, HEAD_DIM))
                run_acc[0, :, cols] = fade * run_acc[0, :, cols] + far_fade * far_acc[
                    :, cols
                ].astype(jnp.float32)

    row = lax.broadcasted_iota(jnp.int32, (tok_rows, HEAD_DIM), 0)
    row_live = row < counts_ref[me]
    for h in range(head_count):
        cols = slice(h * HEAD_DIM, (h + 1) * HEAD_DIM)
        out = jnp.where(row_live, run_acc[0, :, cols] / run_total[0, h], 0.0)
        attended[:, cols] = out.astype(jnp.bfloat16)

    wo_copy.wait()
    theirs = attended[pl.ds(pl.multiple_of((1 - tp) * half, half), half), :]
    mine = attended[pl.ds(pl.multiple_of(tp * half, half), half), :]
    lhs = jnp.concatenate([theirs, mine], axis=0)

    def swap(c):
        return pltpu.make_async_remote_copy(
            src_ref=outgoing.at[c],
            dst_ref=incoming.at[c],
            send_sem=x_send_sem.at[c],
            recv_sem=x_recv_sem.at[c],
            device_id=(me, 1 - tp),
            device_id_type=MESH,
        )

    for c in range(width // chunk):
        part = jnp.dot(
            lhs, wo_all[:, c * chunk : (c + 1) * chunk], preferred_element_type=jnp.float32
        )
        outgoing[c] = part[:half].astype(jnp.bfloat16)
        swap(c).start()
        kept[c] = part[half:]

    def drain(step, carry):
        for p in range(2):

            @pl.when(has_above)
            def _():
                piece(p, UP, step, me - LAYER * step, above).wait_send()

            piece(p, SIDE, step, me - LAYER * step, side_dev).wait_send()
            piece(p, CORE, step, me - LAYER * step, core_dev).wait_send()
            piece(p, CROSS, step, me - LAYER * step, core_dev).wait_send()
        return carry

    lax.fori_loop(0, local + 1, drain, 0)
    if guests:

        @pl.when(is_upper)
        def _():
            ask(guest_slot).wait_send()

        @pl.when(is_host)
        def _():
            def drain_guest(j, carry):
                answer(j, 0).wait_send()
                answer(j, 1).wait_send()
                return carry

            lax.fori_loop(0, guests, drain_guest, 0)

    for c in range(width // chunk):
        swap(c).wait_recv()
        out_ref[:, c * chunk : (c + 1) * chunk] = (
            kept[c] + incoming[c].astype(jnp.float32)
        ).astype(out_ref.dtype)
    for c in range(width // chunk):
        swap(c).wait_send()


def on_device(queries, keys, values, wo, frame_tokens):
    tok_rows, columns = queries.shape
    width = wo.shape[1]
    n = lax.axis_size("ctx")
    half = tok_rows // 2
    chunk = 512 if width % 512 == 0 else width
    chunks = width // chunk
    head_count = columns // HEAD_DIM
    levels = n // LAYER
    guests = levels - group_levels(levels)
    room = max(guests, 1)
    vmem = pltpu.VMEM
    dma = pltpu.SemaphoreType.DMA
    return pl.pallas_call(
        functools.partial(kernel, n, chunk),
        out_shape=jax.ShapeDtypeStruct((half, width), jnp.bfloat16),
        in_specs=[
            pl.BlockSpec(memory_space=pltpu.SMEM),
            pl.BlockSpec(memory_space=vmem),
            pl.BlockSpec(memory_space=pltpu.HBM),
            pl.BlockSpec(memory_space=pltpu.HBM),
            pl.BlockSpec(memory_space=pltpu.HBM),
        ],
        out_specs=pl.BlockSpec(memory_space=vmem),
        scratch_shapes=[
            vmem((n * tok_rows, columns), jnp.bfloat16),
            vmem((n * tok_rows, columns), jnp.bfloat16),
            vmem(wo.shape, jnp.bfloat16),
            vmem((1 + guests, head_count, tok_rows, HEAD_DIM), jnp.float32),
            vmem((1 + guests, head_count, tok_rows, HEAD_DIM), jnp.float32),
            vmem((1 + guests, tok_rows, columns), jnp.float32),
            vmem((room, tok_rows, columns), jnp.bfloat16),
            vmem((room, tok_rows, columns), jnp.bfloat16),
            vmem((room, tok_rows, HEAD_DIM), jnp.float32),
            vmem((tok_rows, columns), jnp.bfloat16),
            vmem((tok_rows, HEAD_DIM), jnp.float32),
            vmem((tok_rows, columns), jnp.bfloat16),
            vmem((chunks, half, chunk), jnp.float32),
            vmem((chunks, half, chunk), jnp.bfloat16),
            vmem((chunks, half, chunk), jnp.bfloat16),
            dma((4, 2, levels)),
            dma((2, n)),
            dma((2,)),
            dma,
            dma((chunks,)),
            dma((chunks,)),
            dma,
            dma((room,)),
            dma((2, room)),
            dma((2,)),
        ],
        compiler_params=pltpu.CompilerParams(
            collective_id=0, has_side_effects=True, vmem_limit_bytes=67043328
        ),
    )(frame_tokens, queries, keys, values, wo)


def solution(mesh):
    in_specs = (P("ctx", "tp"), P("ctx", "tp"), P("ctx", "tp"), P("tp", None), P())
    out_specs = P(("ctx", "tp"), None)
    return jax.shard_map(
        on_device, mesh=mesh, in_specs=in_specs, out_specs=out_specs, check_vma=False
    )
```

```python
import functools
import math

import jax
import jax.numpy as jnp
from jax import lax
from jax.experimental import pallas as pl
from jax.experimental.pallas import tpu as pltpu
from jax.sharding import PartitionSpec as P

HEAD_DIM = 128
LAYER = 4
NEG = -1e30
MESH = pl.DeviceIdType.MESH
UP, SIDE, CORE, CROSS = 0, 1, 2, 3


def group_levels(levels):
    return levels // 2 if levels % 2 == 0 else levels


def kernel(
    n,
    chunk,
    counts_ref,
    q_ref,
    k_hbm,
    v_hbm,
    wo_hbm,
    out_ref,
    k_all,
    v_all,
    wo_all,
    run_max,
    run_acc,
    guest_q,
    guest_max,
    guest_sum,
    guest_acc,
    guest_stats,
    far_acc,
    far_stats,
    attended,
    kept,
    outgoing,
    incoming,
    send_sem,
    recv_sem,
    local_sem,
    wo_sem,
    x_send_sem,
    x_recv_sem,
    q_send_sem,
    q_recv_sem,
    back_send_sem,
    back_recv_sem,
):
    tok_rows, columns = q_ref.shape
    head_count = columns // HEAD_DIM
    width = wo_hbm.shape[1]
    half = tok_rows // 2
    me = lax.axis_index("ctx")
    tp = lax.axis_index("tp")
    levels = n // LAYER
    group = group_levels(levels)
    guests = levels - group
    level = me // LAYER
    is_upper = level >= group
    local = lax.rem(level, group)
    is_host = level == (group - 1 if guests else levels)
    lane = lax.rem(me, LAYER)
    base = level * LAYER
    side_y = lax.rem(lane + 2, LAYER)
    core_lane = lane + 1 - 2 * lax.rem(lane, 2)
    cross_lane = lax.rem(core_lane + 2, LAYER)
    above = lax.rem(me + LAYER, n)
    below = lax.rem(me + n - LAYER, n)
    has_above = local < group - 1
    has_below = local > 0
    host = (group - 1) * LAYER + lane
    guest_slot = lax.rem(level, group)
    side_dev, core_dev = base + side_y, base + core_lane
    halls = (k_all, v_all)
    inputs = (k_hbm, v_hbm)

    wo_copy = pltpu.make_async_copy(wo_hbm, wo_all, wo_sem)
    wo_copy.start()

    def rows_of(src):
        return pl.ds(pl.multiple_of(src * tok_rows, tok_rows), tok_rows)

    own = [
        pltpu.make_async_copy(inputs[p], halls[p].at[rows_of(me)], local_sem.at[p])
        for p in range(2)
    ]
    for p in range(2):
        own[p].start()

    barrier = pltpu.get_barrier_semaphore()

    def greet(dev, other_tp):
        pl.semaphore_signal(barrier, inc=1, device_id=(dev, other_tp), device_id_type=MESH)

    @pl.when(has_above)
    def _():
        greet(above, tp)

    @pl.when(has_below)
    def _():
        greet(below, tp)

    greet(side_dev, tp)
    greet(core_dev, tp)
    greet(me, 1 - tp)

    @pl.when(is_upper)
    def _():
        greet(host, tp)

    @pl.when(is_host)
    def _():
        def greet_guest(j, carry):
            greet(me + LAYER * (1 + j), tp)
            return carry

        lax.fori_loop(0, guests, greet_guest, 0)

    pl.semaphore_wait(
        barrier,
        3
        + has_above.astype(jnp.int32)
        + has_below.astype(jnp.int32)
        + is_upper.astype(jnp.int32)
        + guests * is_host.astype(jnp.int32),
    )

    def ask(j):
        return pltpu.make_async_remote_copy(
            src_ref=q_ref,
            dst_ref=guest_q.at[rows_of(j)],
            send_sem=q_send_sem,
            recv_sem=q_recv_sem.at[j],
            device_id=(host, tp),
            device_id_type=MESH,
        )

    def answer(j, p):
        source, target = ((guest_acc.at[j], far_acc), (guest_stats.at[j], far_stats))[p]
        return pltpu.make_async_remote_copy(
            src_ref=source,
            dst_ref=target,
            send_sem=back_send_sem.at[p, j],
            recv_sem=back_recv_sem.at[p],
            device_id=(lax.rem(me + LAYER * (1 + j), n), tp),
            device_id_type=MESH,
        )

    if guests:

        @pl.when(is_upper)
        def _():
            ask(guest_slot).start()

    def piece(p, kind, step, src, dev):
        return pltpu.make_async_remote_copy(
            src_ref=halls[p].at[rows_of(src)],
            dst_ref=halls[p].at[rows_of(src)],
            send_sem=send_sem.at[kind, p, step],
            recv_sem=recv_sem.at[p, src],
            device_id=(dev, tp),
            device_id_type=MESH,
        )

    def forward_chain(step):
        src = me - LAYER * step
        for p in range(2):

            @pl.when(step > 0)
            def _():
                piece(p, UP, step, src, above).wait_recv()

            @pl.when(step == 0)
            def _():
                own[p].wait()

            @pl.when(has_above)
            def _():
                piece(p, UP, step, src, above).start()

            piece(p, SIDE, step, src, side_dev).start()
            piece(p, CORE, step, src, core_dev).start()

    def forward_side(step):
        src = base + side_y - LAYER * step
        for p in range(2):
            piece(p, CROSS, step, src, core_dev).wait_recv()
            piece(p, CROSS, step, src, core_dev).start()

    def wait_core(step):
        for p in range(2):
            for other in (core_lane, cross_lane):
                piece(p, CORE, step, base + other - LAYER * step, core_dev).wait_recv()

    span = LAYER * tok_rows
    col = lax.broadcasted_iota(jnp.int32, (1, span), 1)
    slot = col // tok_rows
    place = lax.rem(col, tok_rows)
    scale = math.log2(math.e) / math.sqrt(HEAD_DIM)
    ones = jnp.ones((span, HEAD_DIM), jnp.bfloat16)
    head_cols = [slice(h * HEAD_DIM, (h + 1) * HEAD_DIM) for h in range(head_count)]

    def attend(step, query, max_ref, acc_ref, rows, causal):
        first = base - LAYER * step
        limit = jnp.zeros((1, span), jnp.int32)
        for f in range(LAYER):
            live = counts_ref[first + f]
            if causal:
                live = jnp.where(first + f <= me, live, 0)
            limit = jnp.where(slot == f, live, limit)
        allowed = place < limit
        keys_at = pl.ds(pl.multiple_of(first * tok_rows, span), span)
        scores = [
            lax.dot_general(
                query(cols),
                k_all[keys_at, cols],
                (((1,), (1,)), ((), ())),
                preferred_element_type=jnp.float32,
            )
            for cols in head_cols
        ]
        scores = [jnp.where(allowed, one, NEG) for one in scores]
        old_max = [max_ref[h, rows, :][:, :1] for h in range(head_count)]
        new_max = [
            jnp.maximum(old, jnp.max(one, axis=-1, keepdims=True))
            for old, one in zip(old_max, scores)
        ]
        weights = [
            jnp.exp2((one - top) * scale).astype(jnp.bfloat16)
            for one, top in zip(scores, new_max)
        ]
        added = [
            jnp.dot(
                one,
                jnp.concatenate([v_all[keys_at, cols], ones], axis=1),
                preferred_element_type=jnp.float32,
            )
            for one, cols in zip(weights, head_cols)
        ]
        for h in range(head_count):
            fade = jnp.exp2((old_max[h] - new_max[h]) * scale)
            max_ref[h, rows, :] = jnp.broadcast_to(new_max[h], (fade.shape[0], HEAD_DIM))
            acc_ref[h, rows, :] = fade * acc_ref[h, rows, :] + added[h]

    def attend_own(step):
        attend(step, lambda cols: q_ref[:, cols], run_max, run_acc, slice(0, tok_rows), True)

    spot = lax.broadcasted_iota(jnp.int32, (tok_rows, HEAD_DIM), 1)
    pack = 2 if guests % 2 == 0 else 1

    def attend_guests(step, last):
        if not guests:
            return

        @pl.when(is_host)
        def _():
            def one(i, carry):
                block = guests // pack - 1 - i

                @pl.when(step == 0)
                def _():
                    for g in range(pack):
                        ask(block * pack + g).wait_recv()

                rows = pl.ds(pl.multiple_of(block * pack * tok_rows, tok_rows), pack * tok_rows)
                attend(
                    step, lambda cols: guest_q[rows, cols], guest_max, guest_sum, rows, False
                )
                if last:
                    for g in reversed(range(pack)):
                        j = block * pack + g
                        at = rows_of(j)
                        stats = jnp.zeros((tok_rows, HEAD_DIM), jnp.float32)
                        for h in range(head_count):
                            stats = jnp.where(spot == h, guest_max[h, at, :], stats)
                            stats = jnp.where(
                                spot == head_count + h, guest_sum[h, at, HEAD_DIM:], stats
                            )
                            guest_acc[j, :, head_cols[h]] = guest_sum[h, at, :HEAD_DIM].astype(
                                jnp.bfloat16
                            )
                        guest_stats[j] = stats
                        answer(j, 0).start()
                        answer(j, 1).start()
                return carry

            lax.fori_loop(0, guests // pack, one, 0)

    run_max[...] = jnp.full(run_max.shape, NEG, jnp.float32)
    run_acc[...] = jnp.zeros(run_acc.shape, jnp.float32)

    @pl.when(is_host)
    def _():
        guest_max[...] = jnp.full(guest_max.shape, NEG, jnp.float32)
        guest_sum[...] = jnp.zeros(guest_sum.shape, jnp.float32)

    forward_chain(0)
    forward_side(0)

    def body(step, carry):
        forward_chain(step)
        wait_core(step - 1)
        attend_own(step - 1)
        forward_side(step)
        attend_guests(step - 1, False)
        return carry

    lax.fori_loop(1, local + 1, body, 0)
    wait_core(local)
    attend_guests(local, True)
    attend_own(local)

    if guests:

        @pl.when(is_upper)
        def _():
            answer(0, 1).wait_recv()
            answer(0, 0).wait_recv()
            for h in range(head_count):
                far_max = far_stats[:, h : h + 1]
                far_total = far_stats[:, head_count + h : head_count + h + 1]
                old_max = run_max[h][:, :1]
                new_max = jnp.maximum(old_max, far_max)
                fade = jnp.exp2((old_max - new_max) * scale)
                far_fade = jnp.exp2((far_max - new_max) * scale)
                far = jnp.concatenate(
                    [
                        far_acc[:, head_cols[h]].astype(jnp.float32),
                        jnp.broadcast_to(far_total, (tok_rows, HEAD_DIM)),
                    ],
                    axis=1,
                )
                run_acc[h] = fade * run_acc[h] + far_fade * far

    row = lax.broadcasted_iota(jnp.int32, (tok_rows, HEAD_DIM), 0)
    row_live = row < counts_ref[me]
    for h in range(head_count):
        out = jnp.where(row_live, run_acc[h, :, :HEAD_DIM] / run_acc[h, :, HEAD_DIM:], 0.0)
        attended[:, head_cols[h]] = out.astype(jnp.bfloat16)

    wo_copy.wait()
    theirs = attended[pl.ds(pl.multiple_of((1 - tp) * half, half), half), :]
    mine = attended[pl.ds(pl.multiple_of(tp * half, half), half), :]
    lhs = jnp.concatenate([theirs, mine], axis=0)

    def swap(c):
        return pltpu.make_async_remote_copy(
            src_ref=outgoing.at[c],
            dst_ref=incoming.at[c],
            send_sem=x_send_sem.at[c],
            recv_sem=x_recv_sem.at[c],
            device_id=(me, 1 - tp),
            device_id_type=MESH,
        )

    for c in range(width // chunk):
        part = jnp.dot(
            lhs, wo_all[:, c * chunk : (c + 1) * chunk], preferred_element_type=jnp.float32
        )
        outgoing[c] = part[:half].astype(jnp.bfloat16)
        swap(c).start()
        kept[c] = part[half:]

    def drain(step, carry):
        for p in range(2):

            @pl.when(has_above)
            def _():
                piece(p, UP, step, me - LAYER * step, above).wait_send()

            piece(p, SIDE, step, me - LAYER * step, side_dev).wait_send()
            piece(p, CORE, step, me - LAYER * step, core_dev).wait_send()
            piece(p, CROSS, step, me - LAYER * step, core_dev).wait_send()
        return carry

    lax.fori_loop(0, local + 1, drain, 0)
    if guests:

        @pl.when(is_upper)
        def _():
            ask(guest_slot).wait_send()

        @pl.when(is_host)
        def _():
            def drain_guest(j, carry):
                answer(j, 0).wait_send()
                answer(j, 1).wait_send()
                return carry

            lax.fori_loop(0, guests, drain_guest, 0)

    for c in range(width // chunk):
        swap(c).wait_recv()
        out_ref[:, c * chunk : (c + 1) * chunk] = (
            kept[c] + incoming[c].astype(jnp.float32)
        ).astype(out_ref.dtype)
    for c in range(width // chunk):
        swap(c).wait_send()


def on_device(queries, keys, values, wo, frame_tokens):
    tok_rows, columns = queries.shape
    width = wo.shape[1]
    n = lax.axis_size("ctx")
    half = tok_rows // 2
    chunk = 512 if width % 512 == 0 else width
    chunks = width // chunk
    head_count = columns // HEAD_DIM
    levels = n // LAYER
    guests = levels - group_levels(levels)
    room = max(guests, 1)
    vmem = pltpu.VMEM
    dma = pltpu.SemaphoreType.DMA
    return pl.pallas_call(
        functools.partial(kernel, n, chunk),
        out_shape=jax.ShapeDtypeStruct((half, width), jnp.bfloat16),
        in_specs=[
            pl.BlockSpec(memory_space=pltpu.SMEM),
            pl.BlockSpec(memory_space=vmem),
            pl.BlockSpec(memory_space=pltpu.HBM),
            pl.BlockSpec(memory_space=pltpu.HBM),
            pl.BlockSpec(memory_space=pltpu.HBM),
        ],
        out_specs=pl.BlockSpec(memory_space=vmem),
        scratch_shapes=[
            vmem((n * tok_rows, columns), jnp.bfloat16),
            vmem((n * tok_rows, columns), jnp.bfloat16),
            vmem(wo.shape, jnp.bfloat16),
            vmem((head_count, tok_rows, HEAD_DIM), jnp.float32),
            vmem((head_count, tok_rows, 2 * HEAD_DIM), jnp.float32),
            vmem((room * tok_rows, columns), jnp.bfloat16),
            vmem((head_count, room * tok_rows, HEAD_DIM), jnp.float32),
            vmem((head_count, room * tok_rows, 2 * HEAD_DIM), jnp.float32),
            vmem((room, tok_rows, columns), jnp.bfloat16),
            vmem((room, tok_rows, HEAD_DIM), jnp.float32),
            vmem((tok_rows, columns), jnp.bfloat16),
            vmem((tok_rows, HEAD_DIM), jnp.float32),
            vmem((tok_rows, columns), jnp.bfloat16),
            vmem((chunks, half, chunk), jnp.float32),
            vmem((chunks, half, chunk), jnp.bfloat16),
            vmem((chunks, half, chunk), jnp.bfloat16),
            dma((4, 2, levels)),
            dma((2, n)),
            dma((2,)),
            dma,
            dma((chunks,)),
            dma((chunks,)),
            dma,
            dma((room,)),
            dma((2, room)),
            dma((2,)),
        ],
        compiler_params=pltpu.CompilerParams(
            collective_id=0, has_side_effects=True, vmem_limit_bytes=52 << 20
        ),
    )(*[pltpu.with_memory_space_constraint(x, pltpu.HBM) for x in (frame_tokens, queries, keys, values, wo)])


def solution(mesh):
    in_specs = (P("ctx", "tp"), P("ctx", "tp"), P("ctx", "tp"), P("tp", None), P())
    out_specs = P(("ctx", "tp"), None)
    return jax.shard_map(
        on_device, mesh=mesh, in_specs=in_specs, out_specs=out_specs, check_vma=False
    )
```

```python
import functools
import math

import jax
import jax.numpy as jnp
from jax import lax
from jax.experimental import pallas as pl
from jax.experimental.pallas import tpu as pltpu
from jax.sharding import PartitionSpec as P

HEAD_DIM = 128
LAYER = 4
NEG = -1e30
MESH = pl.DeviceIdType.MESH
KEYS, VALUES = 0, 1
UP, SIDE, CORE, CROSS, UP_SIDE = 0, 1, 2, 3, 4


def group_levels(levels):
    return levels // 2 if levels % 2 == 0 else levels


def kernel(
    n,
    chunk,
    counts_ref,
    q_ref,
    k_hbm,
    v_hbm,
    wo_hbm,
    out_ref,
    k_all,
    v_all,
    wo_all,
    run_max,
    run_acc,
    guest_q,
    guest_max,
    guest_sum,
    guest_acc,
    guest_stats,
    far_acc,
    far_stats,
    attended,
    kept,
    outgoing,
    incoming,
    send_sem,
    recv_sem,
    local_sem,
    wo_sem,
    x_send_sem,
    x_recv_sem,
    q_send_sem,
    q_recv_sem,
    back_send_sem,
    back_recv_sem,
):
    tok_rows, columns = q_ref.shape
    head_count = columns // HEAD_DIM
    width = wo_hbm.shape[1]
    half = tok_rows // 2
    me = lax.axis_index("ctx")
    tp = lax.axis_index("tp")
    levels = n // LAYER
    group = group_levels(levels)
    guests = levels - group
    level = me // LAYER
    is_upper = level >= group
    local = lax.rem(level, group)
    is_host = level == (group - 1 if guests else levels)
    lane = lax.rem(me, LAYER)
    base = level * LAYER
    side_y = lax.rem(lane + 2, LAYER)
    core_lane = lane + 1 - 2 * lax.rem(lane, 2)
    cross_lane = lax.rem(core_lane + 2, LAYER)
    above = lax.rem(me + LAYER, n)
    below = lax.rem(me + n - LAYER, n)
    has_above = local < group - 1
    has_below = local > 0
    host = (group - 1) * LAYER + lane
    guest_slot = lax.rem(level, group)
    side_dev, core_dev = base + side_y, base + core_lane
    halls = (k_all, v_all)
    inputs = (k_hbm, v_hbm)

    wo_copy = pltpu.make_async_copy(wo_hbm, wo_all, wo_sem)
    wo_copy.start()

    def rows_of(src):
        return pl.ds(pl.multiple_of(src * tok_rows, tok_rows), tok_rows)

    own = [
        pltpu.make_async_copy(inputs[p], halls[p].at[rows_of(me)], local_sem.at[p])
        for p in range(2)
    ]
    for p in range(2):
        own[p].start()

    barrier = pltpu.get_barrier_semaphore()

    def greet(dev, other_tp):
        pl.semaphore_signal(barrier, inc=1, device_id=(dev, other_tp), device_id_type=MESH)

    @pl.when(has_above)
    def _():
        greet(above, tp)

    @pl.when(has_below)
    def _():
        greet(below, tp)

    greet(side_dev, tp)
    greet(core_dev, tp)
    greet(me, 1 - tp)

    @pl.when(is_upper)
    def _():
        greet(host, tp)

    @pl.when(is_host)
    def _():
        def greet_guest(j, carry):
            greet(me + LAYER * (1 + j), tp)
            return carry

        lax.fori_loop(0, guests, greet_guest, 0)

    pl.semaphore_wait(
        barrier,
        3
        + has_above.astype(jnp.int32)
        + has_below.astype(jnp.int32)
        + is_upper.astype(jnp.int32)
        + guests * is_host.astype(jnp.int32),
    )

    def ask(j):
        return pltpu.make_async_remote_copy(
            src_ref=q_ref,
            dst_ref=guest_q.at[rows_of(j)],
            send_sem=q_send_sem,
            recv_sem=q_recv_sem.at[j],
            device_id=(host, tp),
            device_id_type=MESH,
        )

    def answer(j, p):
        source, target = ((guest_acc.at[j], far_acc), (guest_stats.at[j], far_stats))[p]
        return pltpu.make_async_remote_copy(
            src_ref=source,
            dst_ref=target,
            send_sem=back_send_sem.at[p, j],
            recv_sem=back_recv_sem.at[p],
            device_id=(lax.rem(me + LAYER * (1 + j), n), tp),
            device_id_type=MESH,
        )

    if guests:

        @pl.when(is_upper)
        def _():
            ask(guest_slot).start()

    def piece(p, kind, step, src, dev):
        return pltpu.make_async_remote_copy(
            src_ref=halls[p].at[rows_of(src)],
            dst_ref=halls[p].at[rows_of(src)],
            send_sem=send_sem.at[kind, p, step],
            recv_sem=recv_sem.at[p, src],
            device_id=(dev, tp),
            device_id_type=MESH,
        )

    def send_own():
        for p in (VALUES, KEYS):
            own[p].wait()

            @pl.when(has_above)
            def _():
                piece(p, UP, 0, me, above).start()

        for p in (KEYS, VALUES):
            piece(p, SIDE, 0, me, side_dev).start()
            piece(p, CORE, 0, me, core_dev).start()

    def forward_chain(p, step):
        src = me - LAYER * step
        piece(p, UP, step, src, above).wait_recv()

        @pl.when(has_above)
        def _():
            piece(p, UP, step, src, above).start()

        if p == VALUES:
            piece(p, SIDE, step, src, side_dev).start()
        piece(p, CORE, step, src, core_dev).start()

    def forward_side(p, step):
        src = base + side_y - LAYER * step
        piece(p, CROSS, step, src, core_dev).wait_recv()
        if p == KEYS:

            @pl.when(has_above)
            def _():
                piece(p, UP_SIDE, step, src, above).start()

        piece(p, CROSS, step, src, core_dev).start()

    def wait_core(step):
        for p in range(2):
            for other in (core_lane, cross_lane):
                piece(p, CORE, step, base + other - LAYER * step, core_dev).wait_recv()

    span = LAYER * tok_rows
    col = lax.broadcasted_iota(jnp.int32, (1, span), 1)
    slot = col // tok_rows
    place = lax.rem(col, tok_rows)
    scale = math.log2(math.e) / math.sqrt(HEAD_DIM)
    ones = jnp.ones((span, HEAD_DIM), jnp.bfloat16)
    head_cols = [slice(h * HEAD_DIM, (h + 1) * HEAD_DIM) for h in range(head_count)]

    def attend(step, query, max_ref, acc_ref, rows, causal):
        first = base - LAYER * step
        limit = jnp.zeros((1, span), jnp.int32)
        for f in range(LAYER):
            live = counts_ref[first + f]
            if causal:
                live = jnp.where(first + f <= me, live, 0)
            limit = jnp.where(slot == f, live, limit)
        allowed = place < limit
        keys_at = pl.ds(pl.multiple_of(first * tok_rows, span), span)
        scores = [
            lax.dot_general(
                query(cols),
                k_all[keys_at, cols],
                (((1,), (1,)), ((), ())),
                preferred_element_type=jnp.float32,
            )
            for cols in head_cols
        ]
        scores = [jnp.where(allowed, one, NEG) for one in scores]
        old_max = [max_ref[h, rows, :][:, :1] for h in range(head_count)]
        new_max = [
            jnp.maximum(old, jnp.max(one, axis=-1, keepdims=True))
            for old, one in zip(old_max, scores)
        ]
        weights = [
            jnp.exp2((one - top) * scale).astype(jnp.bfloat16)
            for one, top in zip(scores, new_max)
        ]
        added = [
            jnp.dot(
                one,
                jnp.concatenate([v_all[keys_at, cols], ones], axis=1),
                preferred_element_type=jnp.float32,
            )
            for one, cols in zip(weights, head_cols)
        ]
        for h in range(head_count):
            fade = jnp.exp2((old_max[h] - new_max[h]) * scale)
            max_ref[h, rows, :] = jnp.broadcast_to(new_max[h], (fade.shape[0], HEAD_DIM))
            acc_ref[h, rows, :] = fade * acc_ref[h, rows, :] + added[h]

    def attend_own(step):
        attend(step, lambda cols: q_ref[:, cols], run_max, run_acc, slice(0, tok_rows), True)

    def turn(block):
        missing = jnp.zeros((HEAD_DIM - block.shape[0], HEAD_DIM), jnp.float32)
        return jnp.transpose(jnp.concatenate([block, missing], axis=0))

    spot = lax.broadcasted_iota(jnp.int32, (tok_rows, HEAD_DIM), 1)
    pack = 2 if guests % 2 == 0 else 1

    def attend_guests(step, last):
        if not guests:
            return

        @pl.when(is_host)
        def _():
            def one(i, carry):
                block = guests // pack - 1 - i

                @pl.when(step == 0)
                def _():
                    for g in range(pack):
                        ask(block * pack + g).wait_recv()

                rows = pl.ds(pl.multiple_of(block * pack * tok_rows, tok_rows), pack * tok_rows)
                attend(
                    step, lambda cols: guest_q[rows, cols], guest_max, guest_sum, rows, False
                )
                if last:
                    for g in reversed(range(pack)):
                        j = block * pack + g
                        at = rows_of(j)
                        stats = jnp.zeros((tok_rows, HEAD_DIM), jnp.float32)
                        for h in range(head_count):
                            stats = jnp.where(spot == h, guest_max[h, at, :], stats)
                            stats = jnp.where(
                                spot == head_count + h, guest_sum[h, at, HEAD_DIM:], stats
                            )
                            guest_acc[j, :, head_cols[h]] = guest_sum[h, at, :HEAD_DIM].astype(
                                jnp.bfloat16
                            )
                        guest_stats[j] = turn(stats)[: guest_stats.shape[1]]
                        answer(j, 0).start()
                        answer(j, 1).start()
                return carry

            lax.fori_loop(0, guests // pack, one, 0)

    run_max[...] = jnp.full(run_max.shape, NEG, jnp.float32)
    run_acc[...] = jnp.zeros(run_acc.shape, jnp.float32)

    @pl.when(is_host)
    def _():
        guest_max[...] = jnp.full(guest_max.shape, NEG, jnp.float32)
        guest_sum[...] = jnp.zeros(guest_sum.shape, jnp.float32)

    send_own()
    forward_side(KEYS, 0)

    def body(step, carry):
        forward_chain(VALUES, step)
        forward_side(VALUES, step - 1)
        forward_chain(KEYS, step)
        wait_core(step - 1)
        attend_own(step - 1)
        forward_side(KEYS, step)
        return carry

    lax.fori_loop(1, local + 1, body, 0)
    forward_side(VALUES, local)

    def early_guests(step, carry):
        attend_guests(step, False)
        return carry

    lax.fori_loop(0, local, early_guests, 0)
    wait_core(local)
    attend_guests(local, True)
    attend_own(local)

    if guests:

        @pl.when(is_upper)
        def _():
            answer(0, 1).wait_recv()
            answer(0, 0).wait_recv()
            stats = turn(far_stats[...])[:tok_rows]
            for h in range(head_count):
                far_max = stats[:, h : h + 1]
                far_total = stats[:, head_count + h : head_count + h + 1]
                old_max = run_max[h][:, :1]
                new_max = jnp.maximum(old_max, far_max)
                fade = jnp.exp2((old_max - new_max) * scale)
                far_fade = jnp.exp2((far_max - new_max) * scale)
                far = jnp.concatenate(
                    [
                        far_acc[:, head_cols[h]].astype(jnp.float32),
                        jnp.broadcast_to(far_total, (tok_rows, HEAD_DIM)),
                    ],
                    axis=1,
                )
                run_acc[h] = fade * run_acc[h] + far_fade * far

    row = lax.broadcasted_iota(jnp.int32, (tok_rows, HEAD_DIM), 0)
    row_live = row < counts_ref[me]
    for h in range(head_count):
        out = jnp.where(row_live, run_acc[h, :, :HEAD_DIM] / run_acc[h, :, HEAD_DIM:], 0.0)
        attended[:, head_cols[h]] = out.astype(jnp.bfloat16)

    wo_copy.wait()
    theirs = attended[pl.ds(pl.multiple_of((1 - tp) * half, half), half), :]
    mine = attended[pl.ds(pl.multiple_of(tp * half, half), half), :]
    lhs = jnp.concatenate([theirs, mine], axis=0)

    def swap(c):
        return pltpu.make_async_remote_copy(
            src_ref=outgoing.at[c],
            dst_ref=incoming.at[c],
            send_sem=x_send_sem.at[c],
            recv_sem=x_recv_sem.at[c],
            device_id=(me, 1 - tp),
            device_id_type=MESH,
        )

    for c in range(width // chunk):
        part = jnp.dot(
            lhs, wo_all[:, c * chunk : (c + 1) * chunk], preferred_element_type=jnp.float32
        )
        outgoing[c] = part[:half].astype(jnp.bfloat16)
        swap(c).start()
        kept[c] = part[half:]

    def drain(step, carry):
        for p in (KEYS, VALUES):

            @pl.when(has_above)
            def _():
                piece(p, UP, step, me, above).wait_send()
                if p == KEYS:
                    piece(p, UP_SIDE, step, me, above).wait_send()

            if p == VALUES:
                piece(p, SIDE, step, me, side_dev).wait_send()
            piece(p, CORE, step, me, core_dev).wait_send()
            piece(p, CROSS, step, me, core_dev).wait_send()
        return carry

    piece(KEYS, SIDE, 0, me, side_dev).wait_send()
    lax.fori_loop(0, local + 1, drain, 0)
    if guests:

        @pl.when(is_upper)
        def _():
            ask(guest_slot).wait_send()

        @pl.when(is_host)
        def _():
            def drain_guest(j, carry):
                answer(j, 0).wait_send()
                answer(j, 1).wait_send()
                return carry

            lax.fori_loop(0, guests, drain_guest, 0)

    for c in range(width // chunk):
        swap(c).wait_recv()
        out_ref[:, c * chunk : (c + 1) * chunk] = (
            kept[c] + incoming[c].astype(jnp.float32)
        ).astype(out_ref.dtype)
    for c in range(width // chunk):
        swap(c).wait_send()


def on_device(queries, keys, values, wo, frame_tokens):
    tok_rows, columns = queries.shape
    width = wo.shape[1]
    n = lax.axis_size("ctx")
    half = tok_rows // 2
    chunk = 512 if width % 512 == 0 else width
    chunks = width // chunk
    head_count = columns // HEAD_DIM
    levels = n // LAYER
    guests = levels - group_levels(levels)
    room = max(guests, 1)
    stat_rows = -(-2 * head_count // 8) * 8
    vmem = pltpu.VMEM
    dma = pltpu.SemaphoreType.DMA
    return pl.pallas_call(
        functools.partial(kernel, n, chunk),
        out_shape=jax.ShapeDtypeStruct((half, width), jnp.bfloat16),
        in_specs=[
            pl.BlockSpec(memory_space=pltpu.SMEM),
            pl.BlockSpec(memory_space=vmem),
            pl.BlockSpec(memory_space=pltpu.HBM),
            pl.BlockSpec(memory_space=pltpu.HBM),
            pl.BlockSpec(memory_space=pltpu.HBM),
        ],
        out_specs=pl.BlockSpec(memory_space=vmem),
        scratch_shapes=[
            vmem((n * tok_rows, columns), jnp.bfloat16),
            vmem((n * tok_rows, columns), jnp.bfloat16),
            vmem(wo.shape, jnp.bfloat16),
            vmem((head_count, tok_rows, HEAD_DIM), jnp.float32),
            vmem((head_count, tok_rows, 2 * HEAD_DIM), jnp.float32),
            vmem((room * tok_rows, columns), jnp.bfloat16),
            vmem((head_count, room * tok_rows, HEAD_DIM), jnp.float32),
            vmem((head_count, room * tok_rows, 2 * HEAD_DIM), jnp.float32),
            vmem((room, tok_rows, columns), jnp.bfloat16),
            vmem((room, stat_rows, HEAD_DIM), jnp.float32),
            vmem((tok_rows, columns), jnp.bfloat16),
            vmem((stat_rows, HEAD_DIM), jnp.float32),
            vmem((tok_rows, columns), jnp.bfloat16),
            vmem((chunks, half, chunk), jnp.float32),
            vmem((chunks, half, chunk), jnp.bfloat16),
            vmem((chunks, half, chunk), jnp.bfloat16),
            dma((5, 2, levels)),
            dma((2, n)),
            dma((2,)),
            dma,
            dma((chunks,)),
            dma((chunks,)),
            dma,
            dma((room,)),
            dma((2, room)),
            dma((2,)),
        ],
        compiler_params=pltpu.CompilerParams(
            collective_id=0, has_side_effects=True, vmem_limit_bytes=52 << 20
        ),
    )(*[pltpu.with_memory_space_constraint(x, pltpu.HBM) for x in (frame_tokens, queries, keys, values, wo)])


def solution(mesh):
    in_specs = (P("ctx", "tp"), P("ctx", "tp"), P("ctx", "tp"), P("tp", None), P())
    out_specs = P(("ctx", "tp"), None)
    return jax.shard_map(
        on_device, mesh=mesh, in_specs=in_specs, out_specs=out_specs, check_vma=False
    )
```

```python
import functools
import math

import jax
import jax.numpy as jnp
from jax import lax
from jax.experimental import pallas as pl
from jax.experimental.pallas import tpu as pltpu
from jax.sharding import PartitionSpec as P

HEAD_DIM = 128
LAYER = 4
NEG = -1e30
MESH = pl.DeviceIdType.MESH
KEYS, VALUES = 0, 1
UP, SIDE, CORE, CROSS, UP_SIDE = 0, 1, 2, 3, 4


def group_levels(levels):
    return levels // 2 if levels % 2 == 0 else levels


def wings_of(head_count):
    return 2 if head_count % 2 == 0 else 1


def kernel(
    n,
    chunk,
    counts_ref,
    q_hbm,
    k_hbm,
    v_hbm,
    wo_hbm,
    out_ref,
    q_ref,
    q_sem,
    k_all,
    v_all,
    wo_all,
    run_max,
    run_acc,
    guest_q,
    guest_max,
    guest_sum,
    guest_acc,
    guest_stats,
    far_acc,
    far_stats,
    attended,
    kept,
    outgoing,
    incoming,
    send_sem,
    recv_sem,
    local_sem,
    wo_sem,
    x_send_sem,
    x_recv_sem,
    q_send_sem,
    q_recv_sem,
    back_send_sem,
    back_recv_sem,
):
    tok_rows, columns = q_hbm.shape
    wings = wings_of(columns // HEAD_DIM)
    breadth = columns // wings
    last_wing = wings - 1
    head_count = columns // HEAD_DIM
    width = wo_hbm.shape[1]
    half = tok_rows // 2
    me = lax.axis_index("ctx")
    tp = lax.axis_index("tp")
    levels = n // LAYER
    group = group_levels(levels)
    guests = levels - group
    level = me // LAYER
    is_upper = level >= group
    local = lax.rem(level, group)
    is_host = level == (group - 1 if guests else levels)
    lane = lax.rem(me, LAYER)
    base = level * LAYER
    side_y = lax.rem(lane + 2, LAYER)
    core_lane = lane + 1 - 2 * lax.rem(lane, 2)
    cross_lane = lax.rem(core_lane + 2, LAYER)
    above = lax.rem(me + LAYER, n)
    below = lax.rem(me + n - LAYER, n)
    has_above = local < group - 1
    has_below = local > 0
    host = (group - 1) * LAYER + lane
    guest_slot = lax.rem(level, group)
    side_dev, core_dev = base + side_y, base + core_lane
    halls = (k_all, v_all)
    inputs = (k_hbm, v_hbm)

    wo_copy = pltpu.make_async_copy(wo_hbm, wo_all, wo_sem)
    wo_copy.start()

    def rows_of(src):
        return pl.ds(pl.multiple_of(src * tok_rows, tok_rows), tok_rows)

    q_copy = pltpu.make_async_copy(q_hbm, q_ref, q_sem)
    q_copy.start()

    def wing_cols(w):
        return slice(w * breadth, (w + 1) * breadth)

    own = [
        pltpu.make_async_copy(inputs[p], halls[p].at[rows_of(me)], local_sem.at[p])
        for p in range(2)
    ]
    for p in range(2):
        own[p].start()

    barrier = pltpu.get_barrier_semaphore()

    def greet(dev, other_tp):
        pl.semaphore_signal(barrier, inc=1, device_id=(dev, other_tp), device_id_type=MESH)

    @pl.when(has_above)
    def _():
        greet(above, tp)

    @pl.when(has_below)
    def _():
        greet(below, tp)

    greet(side_dev, tp)
    greet(core_dev, tp)
    greet(me, 1 - tp)

    @pl.when(is_upper)
    def _():
        greet(host, tp)

    @pl.when(is_host)
    def _():
        def greet_guest(j, carry):
            greet(me + LAYER * (1 + j), tp)
            return carry

        lax.fori_loop(0, guests, greet_guest, 0)

    pl.semaphore_wait(
        barrier,
        3
        + has_above.astype(jnp.int32)
        + has_below.astype(jnp.int32)
        + is_upper.astype(jnp.int32)
        + guests * is_host.astype(jnp.int32),
    )

    def ask(j, w):
        return pltpu.make_async_remote_copy(
            src_ref=q_ref.at[:, wing_cols(w)],
            dst_ref=guest_q.at[rows_of(j), wing_cols(w)],
            send_sem=q_send_sem.at[w],
            recv_sem=q_recv_sem.at[w, j],
            device_id=(host, tp),
            device_id_type=MESH,
        )

    def answer(j, p, w):
        source, target = (
            (guest_acc.at[j, :, wing_cols(w)], far_acc.at[:, wing_cols(w)]),
            (guest_stats.at[j, w], far_stats.at[w]),
        )[p]
        return pltpu.make_async_remote_copy(
            src_ref=source,
            dst_ref=target,
            send_sem=back_send_sem.at[p, w, j],
            recv_sem=back_recv_sem.at[p, w],
            device_id=(lax.rem(me + LAYER * (1 + j), n), tp),
            device_id_type=MESH,
        )

    q_copy.wait()
    if guests:

        @pl.when(is_upper)
        def _():
            for w in range(wings):
                ask(guest_slot, w).start()

    def piece(p, w, kind, step, src, dev):
        where = halls[p].at[rows_of(src), wing_cols(w)]
        return pltpu.make_async_remote_copy(
            src_ref=where,
            dst_ref=where,
            send_sem=send_sem.at[kind, p * wings + w, step],
            recv_sem=recv_sem.at[p * wings + w, src],
            device_id=(dev, tp),
            device_id_type=MESH,
        )

    def rise_own(p, w):
        @pl.when(has_above)
        def _():
            piece(p, w, UP, 0, me, above).start()

    def forward_chain(p, w, step):
        src = me - LAYER * step
        piece(p, w, UP, step, src, above).wait_recv()

        @pl.when(has_above)
        def _():
            piece(p, w, UP, step, src, above).start()

        if p == VALUES:
            piece(p, w, SIDE, step, src, side_dev).start()
        piece(p, w, CORE, step, src, core_dev).start()

    def forward_side(p, w, step):
        src = base + side_y - LAYER * step
        piece(p, w, CROSS, step, src, core_dev).wait_recv()
        if p == KEYS:

            @pl.when(has_above)
            def _():
                piece(p, w, UP_SIDE, step, src, above).start()

        piece(p, w, CROSS, step, src, core_dev).start()

    def wait_core(w, step):
        for p in range(2):
            for other in (core_lane, cross_lane):
                piece(p, w, CORE, step, base + other - LAYER * step, core_dev).wait_recv()

    span = LAYER * tok_rows
    col = lax.broadcasted_iota(jnp.int32, (1, span), 1)
    slot = col // tok_rows
    place = lax.rem(col, tok_rows)
    scale = math.log2(math.e) / math.sqrt(HEAD_DIM)
    ones = jnp.ones((span, HEAD_DIM), jnp.bfloat16)
    head_cols = [slice(h * HEAD_DIM, (h + 1) * HEAD_DIM) for h in range(head_count)]

    each = head_count // wings
    wing_heads = [range(w * each, (w + 1) * each) for w in range(wings)]

    def attend(step, query, max_ref, acc_ref, rows, causal, w):
        heads = wing_heads[w]
        cols_of = [head_cols[h] for h in heads]
        first = base - LAYER * step
        limit = jnp.zeros((1, span), jnp.int32)
        for f in range(LAYER):
            live = counts_ref[first + f]
            if causal:
                live = jnp.where(first + f <= me, live, 0)
            limit = jnp.where(slot == f, live, limit)
        allowed = place < limit
        keys_at = pl.ds(pl.multiple_of(first * tok_rows, span), span)
        scores = [
            lax.dot_general(
                query(cols),
                k_all[keys_at, cols],
                (((1,), (1,)), ((), ())),
                preferred_element_type=jnp.float32,
            )
            for cols in cols_of
        ]
        scores = [jnp.where(allowed, one, NEG) for one in scores]
        old_max = [max_ref[h, rows, :][:, :1] for h in heads]
        new_max = [
            jnp.maximum(old, jnp.max(one, axis=-1, keepdims=True))
            for old, one in zip(old_max, scores)
        ]
        weights = [
            jnp.exp2((one - top) * scale).astype(jnp.bfloat16)
            for one, top in zip(scores, new_max)
        ]
        added = [
            jnp.dot(
                one,
                jnp.concatenate([v_all[keys_at, cols], ones], axis=1),
                preferred_element_type=jnp.float32,
            )
            for one, cols in zip(weights, cols_of)
        ]
        for i, h in enumerate(heads):
            fade = jnp.exp2((old_max[i] - new_max[i]) * scale)
            max_ref[h, rows, :] = jnp.broadcast_to(new_max[i], (fade.shape[0], HEAD_DIM))
            acc_ref[h, rows, :] = fade * acc_ref[h, rows, :] + added[i]

    def attend_own(step, w):
        attend(step, lambda cols: q_ref[:, cols], run_max, run_acc, slice(0, tok_rows), True, w)

    def turn(block):
        missing = jnp.zeros((HEAD_DIM - block.shape[0], HEAD_DIM), jnp.float32)
        return jnp.transpose(jnp.concatenate([block, missing], axis=0))

    spot = lax.broadcasted_iota(jnp.int32, (tok_rows, HEAD_DIM), 1)
    pack = 2 if guests % 2 == 0 else 1

    def attend_guests(step, last, w):
        if not guests:
            return

        @pl.when(is_host)
        def _():
            def one(i, carry):
                block = guests // pack - 1 - i

                @pl.when(step == 0)
                def _():
                    for g in range(pack):
                        ask(block * pack + g, w).wait_recv()

                rows = pl.ds(pl.multiple_of(block * pack * tok_rows, tok_rows), pack * tok_rows)
                attend(
                    step, lambda cols: guest_q[rows, cols], guest_max, guest_sum, rows, False, w
                )
                if last:
                    for g in reversed(range(pack)):
                        j = block * pack + g
                        at = rows_of(j)
                        stats = jnp.zeros((tok_rows, HEAD_DIM), jnp.float32)
                        for i, h in enumerate(wing_heads[w]):
                            stats = jnp.where(spot == i, guest_max[h, at, :], stats)
                            stats = jnp.where(
                                spot == each + i, guest_sum[h, at, HEAD_DIM:], stats
                            )
                            guest_acc[j, :, head_cols[h]] = guest_sum[h, at, :HEAD_DIM].astype(
                                jnp.bfloat16
                            )
                        guest_stats[j, w] = turn(stats)[: guest_stats.shape[2]]
                        answer(j, 0, w).start()
                        answer(j, 1, w).start()
                return carry

            lax.fori_loop(0, guests // pack, one, 0)

    run_max[...] = jnp.full(run_max.shape, NEG, jnp.float32)
    run_acc[...] = jnp.zeros(run_acc.shape, jnp.float32)

    @pl.when(is_host)
    def _():
        guest_max[...] = jnp.full(guest_max.shape, NEG, jnp.float32)
        guest_sum[...] = jnp.zeros(guest_sum.shape, jnp.float32)

    for p in (VALUES, KEYS):
        own[p].wait()
    rise_own(VALUES, 0)
    rise_own(KEYS, 0)
    for p in (KEYS, VALUES):
        piece(p, 0, SIDE, 0, me, side_dev).start()
        piece(p, 0, CORE, 0, me, core_dev).start()
    if last_wing:
        rise_own(VALUES, 1)
        piece(KEYS, 1, SIDE, 0, me, side_dev).start()
        for p in (KEYS, VALUES):
            piece(p, 1, CORE, 0, me, core_dev).start()
    forward_side(KEYS, 0, 0)
    if last_wing:
        rise_own(KEYS, 1)

    @pl.when(has_below)
    def _():
        forward_chain(VALUES, 0, 1)

    if last_wing:
        piece(VALUES, 1, SIDE, 0, me, side_dev).start()

    def body(step, carry):
        forward_side(VALUES, 0, step - 1)
        forward_chain(KEYS, 0, step)
        if last_wing:
            forward_side(KEYS, 1, step - 1)
            forward_chain(VALUES, 1, step)
        forward_side(KEYS, 0, step)
        if last_wing:
            forward_chain(KEYS, 1, step)
            forward_side(VALUES, 1, step - 1)

        @pl.when(step < local)
        def _():
            forward_chain(VALUES, 0, step + 1)

        return carry

    lax.fori_loop(1, local + 1, body, 0)

    for w in range(wings):
        forward_side(VALUES, w, local)
        if w:
            forward_side(KEYS, w, local)

        def early(step, carry):
            wait_core(w, step)
            attend_guests(step, False, w)
            return carry

        lax.fori_loop(0, local, early, 0)
        wait_core(w, local)
        attend_guests(local, True, w)

    for w in range(wings):

        def own_step(step, carry):
            attend_own(step, w)
            return carry

        lax.fori_loop(0, local + 1, own_step, 0)

    if guests:

        @pl.when(is_upper)
        def _():
            for w in range(wings):
                answer(0, 0, w).wait_recv()
                answer(0, 1, w).wait_recv()
                stats = turn(far_stats[w])[:tok_rows]
                for i, h in enumerate(wing_heads[w]):
                    far_max = stats[:, i : i + 1]
                    far_total = stats[:, each + i : each + i + 1]
                    old_max = run_max[h][:, :1]
                    new_max = jnp.maximum(old_max, far_max)
                    fade = jnp.exp2((old_max - new_max) * scale)
                    far_fade = jnp.exp2((far_max - new_max) * scale)
                    far = jnp.concatenate(
                        [
                            far_acc[:, head_cols[h]].astype(jnp.float32),
                            jnp.broadcast_to(far_total, (tok_rows, HEAD_DIM)),
                        ],
                        axis=1,
                    )
                    run_acc[h] = fade * run_acc[h] + far_fade * far

    row = lax.broadcasted_iota(jnp.int32, (tok_rows, HEAD_DIM), 0)
    row_live = row < counts_ref[me]
    for h in range(head_count):
        out = jnp.where(row_live, run_acc[h, :, :HEAD_DIM] / run_acc[h, :, HEAD_DIM:], 0.0)
        attended[:, head_cols[h]] = out.astype(jnp.bfloat16)

    wo_copy.wait()
    theirs = attended[pl.ds(pl.multiple_of((1 - tp) * half, half), half), :]
    mine = attended[pl.ds(pl.multiple_of(tp * half, half), half), :]
    lhs = jnp.concatenate([theirs, mine], axis=0)

    def swap(c):
        return pltpu.make_async_remote_copy(
            src_ref=outgoing.at[c],
            dst_ref=incoming.at[c],
            send_sem=x_send_sem.at[c],
            recv_sem=x_recv_sem.at[c],
            device_id=(me, 1 - tp),
            device_id_type=MESH,
        )

    for c in range(width // chunk):
        part = jnp.dot(
            lhs, wo_all[:, c * chunk : (c + 1) * chunk], preferred_element_type=jnp.float32
        )
        outgoing[c] = part[:half].astype(jnp.bfloat16)
        swap(c).start()
        kept[c] = part[half:]

    def drain(step, carry):
        for w in range(wings):
            for p in (KEYS, VALUES):

                @pl.when(has_above)
                def _():
                    piece(p, w, UP, step, me, above).wait_send()
                    if p == KEYS:
                        piece(p, w, UP_SIDE, step, me, above).wait_send()

                if p == VALUES:
                    piece(p, w, SIDE, step, me, side_dev).wait_send()
                piece(p, w, CORE, step, me, core_dev).wait_send()
                piece(p, w, CROSS, step, me, core_dev).wait_send()
        return carry

    for w in range(wings):
        piece(KEYS, w, SIDE, 0, me, side_dev).wait_send()
    lax.fori_loop(0, local + 1, drain, 0)
    if guests:

        @pl.when(is_upper)
        def _():
            for w in range(wings):
                ask(guest_slot, w).wait_send()

        @pl.when(is_host)
        def _():
            def drain_guest(j, carry):
                for w in range(wings):
                    answer(j, 0, w).wait_send()
                    answer(j, 1, w).wait_send()
                return carry

            lax.fori_loop(0, guests, drain_guest, 0)

    for c in range(width // chunk):
        swap(c).wait_recv()
        out_ref[:, c * chunk : (c + 1) * chunk] = (
            kept[c] + incoming[c].astype(jnp.float32)
        ).astype(out_ref.dtype)
    for c in range(width // chunk):
        swap(c).wait_send()


def on_device(queries, keys, values, wo, frame_tokens):
    tok_rows, columns = queries.shape
    width = wo.shape[1]
    n = lax.axis_size("ctx")
    half = tok_rows // 2
    chunk = 256 if width % 256 == 0 else width
    chunks = width // chunk
    head_count = columns // HEAD_DIM
    levels = n // LAYER
    guests = levels - group_levels(levels)
    room = max(guests, 1)
    wings = wings_of(head_count)
    stat_rows = -(-2 * head_count // wings // 8) * 8
    vmem = pltpu.VMEM
    dma = pltpu.SemaphoreType.DMA
    return pl.pallas_call(
        functools.partial(kernel, n, chunk),
        out_shape=jax.ShapeDtypeStruct((half, width), jnp.bfloat16),
        in_specs=[
            pl.BlockSpec(memory_space=pltpu.SMEM),
            pl.BlockSpec(memory_space=pltpu.HBM),
            pl.BlockSpec(memory_space=pltpu.HBM),
            pl.BlockSpec(memory_space=pltpu.HBM),
            pl.BlockSpec(memory_space=pltpu.HBM),
        ],
        out_specs=pl.BlockSpec(memory_space=vmem),
        scratch_shapes=[
            vmem((tok_rows, columns), jnp.bfloat16),
            dma,
            vmem((n * tok_rows, columns), jnp.bfloat16),
            vmem((n * tok_rows, columns), jnp.bfloat16),
            vmem(wo.shape, jnp.bfloat16),
            vmem((head_count, tok_rows, HEAD_DIM), jnp.float32),
            vmem((head_count, tok_rows, 2 * HEAD_DIM), jnp.float32),
            vmem((room * tok_rows, columns), jnp.bfloat16),
            vmem((head_count, room * tok_rows, HEAD_DIM), jnp.float32),
            vmem((head_count, room * tok_rows, 2 * HEAD_DIM), jnp.float32),
            vmem((room, tok_rows, columns), jnp.bfloat16),
            vmem((room, wings, stat_rows, HEAD_DIM), jnp.float32),
            vmem((tok_rows, columns), jnp.bfloat16),
            vmem((wings, stat_rows, HEAD_DIM), jnp.float32),
            vmem((tok_rows, columns), jnp.bfloat16),
            vmem((chunks, half, chunk), jnp.float32),
            vmem((chunks, half, chunk), jnp.bfloat16),
            vmem((chunks, half, chunk), jnp.bfloat16),
            dma((5, 2 * wings, levels)),
            dma((2 * wings, n)),
            dma((2,)),
            dma,
            dma((chunks,)),
            dma((chunks,)),
            dma((wings,)),
            dma((wings, room)),
            dma((2, wings, room)),
            dma((2, wings)),
        ],
        compiler_params=pltpu.CompilerParams(
            collective_id=0, has_side_effects=True, vmem_limit_bytes=52 << 20
        ),
    )(*[pltpu.with_memory_space_constraint(x, pltpu.HBM) for x in (frame_tokens, queries, keys, values, wo)])


def solution(mesh):
    in_specs = (P("ctx", "tp"), P("ctx", "tp"), P("ctx", "tp"), P("tp", None), P())
    out_specs = P(("ctx", "tp"), None)
    return jax.shard_map(
        on_device, mesh=mesh, in_specs=in_specs, out_specs=out_specs, check_vma=False
    )
```

```python
import functools
import math

import jax
import jax.numpy as jnp
from jax import lax
from jax.experimental import pallas as pl
from jax.experimental.pallas import tpu as pltpu
from jax.sharding import PartitionSpec as P

HEAD_DIM = 128
LAYER = 4
NEG = -1e30
MESH = pl.DeviceIdType.MESH
KEYS, VALUES = 0, 1
UP, SIDE, CORE, CROSS, UP_SIDE = 0, 1, 2, 3, 4


def group_levels(levels):
    return levels // 2 if levels % 2 == 0 else levels


def wings_of(head_count):
    return 2 if head_count % 2 == 0 else 1


def kernel(
    n,
    chunk,
    counts_ref,
    q_hbm,
    k_hbm,
    v_hbm,
    wo_hbm,
    out_ref,
    q_ref,
    q_sem,
    k_all,
    v_all,
    wo_all,
    run_max,
    run_acc,
    guest_q,
    guest_max,
    guest_sum,
    guest_acc,
    guest_stats,
    far_acc,
    far_stats,
    attended,
    kept,
    outgoing,
    incoming,
    send_sem,
    recv_sem,
    local_sem,
    wo_sem,
    x_send_sem,
    x_recv_sem,
    q_send_sem,
    q_recv_sem,
    back_send_sem,
    back_recv_sem,
):
    tok_rows, columns = q_hbm.shape
    wings = wings_of(columns // HEAD_DIM)
    breadth = columns // wings
    last_wing = wings - 1
    head_count = columns // HEAD_DIM
    width = wo_hbm.shape[1]
    half = tok_rows // 2
    me = lax.axis_index("ctx")
    tp = lax.axis_index("tp")
    levels = n // LAYER
    group = group_levels(levels)
    guests = levels - group
    level = me // LAYER
    is_upper = level >= group
    local = lax.rem(level, group)
    is_host = level == (group - 1 if guests else levels)
    lane = lax.rem(me, LAYER)
    base = level * LAYER
    side_y = lax.rem(lane + 2, LAYER)
    core_lane = lane + 1 - 2 * lax.rem(lane, 2)
    cross_lane = lax.rem(core_lane + 2, LAYER)
    above = lax.rem(me + LAYER, n)
    below = lax.rem(me + n - LAYER, n)
    has_above = local < group - 1
    has_below = local > 0
    host = (group - 1) * LAYER + lane
    guest_slot = lax.rem(level, group)
    side_dev, core_dev = base + side_y, base + core_lane
    halls = (k_all, v_all)
    inputs = (k_hbm, v_hbm)

    wo_copy = pltpu.make_async_copy(wo_hbm, wo_all, wo_sem)
    wo_copy.start()

    def rows_of(src):
        return pl.ds(pl.multiple_of(src * tok_rows, tok_rows), tok_rows)

    q_copy = pltpu.make_async_copy(q_hbm, q_ref, q_sem)
    q_copy.start()

    def wing_cols(w):
        return slice(w * breadth, (w + 1) * breadth)

    own = [
        pltpu.make_async_copy(inputs[p], halls[p].at[rows_of(me)], local_sem.at[p])
        for p in range(2)
    ]
    for p in range(2):
        own[p].start()

    barrier = pltpu.get_barrier_semaphore()

    def greet(dev, other_tp):
        pl.semaphore_signal(barrier, inc=1, device_id=(dev, other_tp), device_id_type=MESH)

    @pl.when(has_above)
    def _():
        greet(above, tp)

    @pl.when(has_below)
    def _():
        greet(below, tp)

    greet(side_dev, tp)
    greet(core_dev, tp)
    greet(me, 1 - tp)

    @pl.when(is_upper)
    def _():
        greet(host, tp)

    @pl.when(is_host)
    def _():
        def greet_guest(j, carry):
            greet(me + LAYER * (1 + j), tp)
            return carry

        lax.fori_loop(0, guests, greet_guest, 0)

    pl.semaphore_wait(
        barrier,
        3
        + has_above.astype(jnp.int32)
        + has_below.astype(jnp.int32)
        + is_upper.astype(jnp.int32)
        + guests * is_host.astype(jnp.int32),
    )

    def ask(j, w):
        return pltpu.make_async_remote_copy(
            src_ref=q_ref.at[:, wing_cols(w)],
            dst_ref=guest_q.at[rows_of(j), wing_cols(w)],
            send_sem=q_send_sem.at[w],
            recv_sem=q_recv_sem.at[w, j],
            device_id=(host, tp),
            device_id_type=MESH,
        )

    def answer(j, p, w):
        source, target = (
            (guest_acc.at[j, :, wing_cols(w)], far_acc.at[:, wing_cols(w)]),
            (guest_stats.at[j, w], far_stats.at[w]),
        )[p]
        return pltpu.make_async_remote_copy(
            src_ref=source,
            dst_ref=target,
            send_sem=back_send_sem.at[p, w, j],
            recv_sem=back_recv_sem.at[p, w],
            device_id=(lax.rem(me + LAYER * (1 + j), n), tp),
            device_id_type=MESH,
        )

    q_copy.wait()
    if guests:

        @pl.when(is_upper)
        def _():
            for w in range(wings):
                ask(guest_slot, w).start()

    def piece(p, w, kind, step, src, dev):
        where = halls[p].at[rows_of(src), wing_cols(w)]
        return pltpu.make_async_remote_copy(
            src_ref=where,
            dst_ref=where,
            send_sem=send_sem.at[kind, p * wings + w, step],
            recv_sem=recv_sem.at[p * wings + w, src],
            device_id=(dev, tp),
            device_id_type=MESH,
        )

    def rise_own(p, w):
        @pl.when(has_above)
        def _():
            piece(p, w, UP, 0, me, above).start()

    def forward_chain(p, w, step):
        src = me - LAYER * step
        piece(p, w, UP, step, src, above).wait_recv()

        @pl.when(has_above)
        def _():
            piece(p, w, UP, step, src, above).start()

        if p == VALUES:
            piece(p, w, SIDE, step, src, side_dev).start()
        piece(p, w, CORE, step, src, core_dev).start()

    def forward_side(p, w, step):
        src = base + side_y - LAYER * step
        piece(p, w, CROSS, step, src, core_dev).wait_recv()
        if p == KEYS:

            @pl.when(has_above)
            def _():
                piece(p, w, UP_SIDE, step, src, above).start()

        piece(p, w, CROSS, step, src, core_dev).start()

    def wait_core(w, step):
        for p in range(2):
            for other in (core_lane, cross_lane):
                piece(p, w, CORE, step, base + other - LAYER * step, core_dev).wait_recv()

    span = LAYER * tok_rows
    col = lax.broadcasted_iota(jnp.int32, (1, span), 1)
    slot = col // tok_rows
    place = lax.rem(col, tok_rows)
    scale = math.log2(math.e) / math.sqrt(HEAD_DIM)
    ones = jnp.ones((span, HEAD_DIM), jnp.bfloat16)
    head_cols = [slice(h * HEAD_DIM, (h + 1) * HEAD_DIM) for h in range(head_count)]

    each = head_count // wings
    wing_heads = [range(w * each, (w + 1) * each) for w in range(wings)]

    def attend(step, query, max_ref, acc_ref, rows, causal, w):
        heads = wing_heads[w]
        cols_of = [head_cols[h] for h in heads]
        first = base - LAYER * step
        limit = jnp.zeros((1, span), jnp.int32)
        for f in range(LAYER):
            live = counts_ref[first + f]
            if causal:
                live = jnp.where(first + f <= me, live, 0)
            limit = jnp.where(slot == f, live, limit)
        allowed = place < limit
        keys_at = pl.ds(pl.multiple_of(first * tok_rows, span), span)
        scores = [
            lax.dot_general(
                query(cols),
                k_all[keys_at, cols],
                (((1,), (1,)), ((), ())),
                preferred_element_type=jnp.float32,
            )
            for cols in cols_of
        ]
        scores = [jnp.where(allowed, one, NEG) for one in scores]
        old_max = [max_ref[h, rows, :][:, :1] for h in heads]
        new_max = [
            jnp.maximum(old, jnp.max(one, axis=-1, keepdims=True))
            for old, one in zip(old_max, scores)
        ]
        weights = [
            jnp.exp2((one - top) * scale).astype(jnp.bfloat16)
            for one, top in zip(scores, new_max)
        ]
        added = [
            jnp.dot(
                one,
                jnp.concatenate([v_all[keys_at, cols], ones], axis=1),
                preferred_element_type=jnp.float32,
            )
            for one, cols in zip(weights, cols_of)
        ]
        for i, h in enumerate(heads):
            fade = jnp.exp2((old_max[i] - new_max[i]) * scale)
            max_ref[h, rows, :] = jnp.broadcast_to(new_max[i], (fade.shape[0], HEAD_DIM))
            acc_ref[h, rows, :] = fade * acc_ref[h, rows, :] + added[i]

    def attend_own(step, w):
        attend(step, lambda cols: q_ref[:, cols], run_max, run_acc, slice(0, tok_rows), True, w)

    def turn(block):
        missing = jnp.zeros((HEAD_DIM - block.shape[0], HEAD_DIM), jnp.float32)
        return jnp.transpose(jnp.concatenate([block, missing], axis=0))

    spot = lax.broadcasted_iota(jnp.int32, (tok_rows, HEAD_DIM), 1)
    pack = 2 if guests % 2 == 0 else 1

    def attend_guests(step, last, w):
        if not guests:
            return

        @pl.when(is_host)
        def _():
            def one(i, carry):
                block = guests // pack - 1 - i

                @pl.when(step == 0)
                def _():
                    for g in range(pack):
                        ask(block * pack + g, w).wait_recv()

                rows = pl.ds(pl.multiple_of(block * pack * tok_rows, tok_rows), pack * tok_rows)
                attend(
                    step, lambda cols: guest_q[rows, cols], guest_max, guest_sum, rows, False, w
                )
                if last:
                    for g in reversed(range(pack)):
                        j = block * pack + g
                        at = rows_of(j)
                        stats = jnp.zeros((tok_rows, HEAD_DIM), jnp.float32)
                        for i, h in enumerate(wing_heads[w]):
                            stats = jnp.where(spot == i, guest_max[h, at, :], stats)
                            stats = jnp.where(
                                spot == each + i, guest_sum[h, at, HEAD_DIM:], stats
                            )
                            guest_acc[j, :, head_cols[h]] = guest_sum[h, at, :HEAD_DIM].astype(
                                jnp.bfloat16
                            )
                        guest_stats[j, w] = turn(stats)[: guest_stats.shape[2]]
                        answer(j, 0, w).start()
                        answer(j, 1, w).start()
                return carry

            lax.fori_loop(0, guests // pack, one, 0)

    run_max[...] = jnp.full(run_max.shape, NEG, jnp.float32)
    run_acc[...] = jnp.zeros(run_acc.shape, jnp.float32)

    @pl.when(is_host)
    def _():
        guest_max[...] = jnp.full(guest_max.shape, NEG, jnp.float32)
        guest_sum[...] = jnp.zeros(guest_sum.shape, jnp.float32)

    for p in (VALUES, KEYS):
        own[p].wait()
    rise_own(VALUES, 0)
    rise_own(KEYS, 0)
    for p in (KEYS, VALUES):
        piece(p, 0, SIDE, 0, me, side_dev).start()
        piece(p, 0, CORE, 0, me, core_dev).start()
    if last_wing:
        rise_own(VALUES, 1)
        piece(KEYS, 1, SIDE, 0, me, side_dev).start()
        for p in (KEYS, VALUES):
            piece(p, 1, CORE, 0, me, core_dev).start()
    forward_side(KEYS, 0, 0)
    if last_wing:
        rise_own(KEYS, 1)

    @pl.when(has_below)
    def _():
        forward_chain(VALUES, 0, 1)

    if last_wing:
        piece(VALUES, 1, SIDE, 0, me, side_dev).start()

    def body(step, carry):
        forward_side(VALUES, 0, step - 1)
        forward_chain(KEYS, 0, step)
        if last_wing:
            forward_side(KEYS, 1, step - 1)
            forward_chain(VALUES, 1, step)
        forward_side(KEYS, 0, step)
        if last_wing:
            forward_chain(KEYS, 1, step)
            forward_side(VALUES, 1, step - 1)

        @pl.when(step < local)
        def _():
            forward_chain(VALUES, 0, step + 1)

        return carry

    lax.fori_loop(1, local + 1, body, 0)

    for w in range(wings):
        forward_side(VALUES, w, local)
        if w:
            forward_side(KEYS, w, local)

        def early(step, carry):
            wait_core(w, step)
            attend_guests(step, False, w)
            return carry

        lax.fori_loop(0, local, early, 0)
        wait_core(w, local)
        attend_guests(local, True, w)

    for w in range(wings):

        def own_step(step, carry):
            attend_own(step, w)
            return carry

        lax.fori_loop(0, local + 1, own_step, 0)

    if guests:

        @pl.when(is_upper)
        def _():
            for w in range(wings):
                answer(0, 0, w).wait_recv()
                answer(0, 1, w).wait_recv()
                stats = turn(far_stats[w])[:tok_rows]
                for i, h in enumerate(wing_heads[w]):
                    far_max = stats[:, i : i + 1]
                    far_total = stats[:, each + i : each + i + 1]
                    old_max = run_max[h][:, :1]
                    new_max = jnp.maximum(old_max, far_max)
                    fade = jnp.exp2((old_max - new_max) * scale)
                    far_fade = jnp.exp2((far_max - new_max) * scale)
                    far = jnp.concatenate(
                        [
                            far_acc[:, head_cols[h]].astype(jnp.float32),
                            jnp.broadcast_to(far_total, (tok_rows, HEAD_DIM)),
                        ],
                        axis=1,
                    )
                    run_acc[h] = fade * run_acc[h] + far_fade * far

    row = lax.broadcasted_iota(jnp.int32, (tok_rows, HEAD_DIM), 0)
    row_live = row < counts_ref[me]
    for h in range(head_count):
        out = jnp.where(row_live, run_acc[h, :, :HEAD_DIM] / run_acc[h, :, HEAD_DIM:], 0.0)
        attended[:, head_cols[h]] = out.astype(jnp.bfloat16)

    wo_copy.wait()
    theirs = attended[pl.ds(pl.multiple_of((1 - tp) * half, half), half), :]
    mine = attended[pl.ds(pl.multiple_of(tp * half, half), half), :]
    lhs = jnp.concatenate([theirs, mine], axis=0)

    def swap(c):
        return pltpu.make_async_remote_copy(
            src_ref=outgoing.at[c],
            dst_ref=incoming.at[c],
            send_sem=x_send_sem.at[c],
            recv_sem=x_recv_sem.at[c],
            device_id=(me, 1 - tp),
            device_id_type=MESH,
        )

    for c in range(width // chunk):
        part = jnp.dot(
            lhs, wo_all[:, c * chunk : (c + 1) * chunk], preferred_element_type=jnp.float32
        )
        outgoing[c] = part[:half].astype(jnp.bfloat16)
        swap(c).start()
        kept[c] = part[half:]

    def drain(step, carry):
        for w in range(wings):
            for p in (KEYS, VALUES):

                @pl.when(has_above)
                def _():
                    piece(p, w, UP, step, me, above).wait_send()
                    if p == KEYS:
                        piece(p, w, UP_SIDE, step, me, above).wait_send()

                if p == VALUES:
                    piece(p, w, SIDE, step, me, side_dev).wait_send()
                piece(p, w, CORE, step, me, core_dev).wait_send()
                piece(p, w, CROSS, step, me, core_dev).wait_send()
        return carry

    for w in range(wings):
        piece(KEYS, w, SIDE, 0, me, side_dev).wait_send()
    lax.fori_loop(0, local + 1, drain, 0)
    if guests:

        @pl.when(is_upper)
        def _():
            for w in range(wings):
                ask(guest_slot, w).wait_send()

        @pl.when(is_host)
        def _():
            def drain_guest(j, carry):
                for w in range(wings):
                    answer(j, 0, w).wait_send()
                    answer(j, 1, w).wait_send()
                return carry

            lax.fori_loop(0, guests, drain_guest, 0)

    for c in range(width // chunk):
        swap(c).wait_recv()
        out_ref[:, c * chunk : (c + 1) * chunk] = (
            kept[c] + incoming[c].astype(jnp.float32)
        ).astype(out_ref.dtype)
    for c in range(width // chunk):
        swap(c).wait_send()


def on_device(queries, keys, values, wo, frame_tokens):
    tok_rows, columns = queries.shape
    width = wo.shape[1]
    n = lax.axis_size("ctx")
    half = tok_rows // 2
    chunk = 512 if width % 512 == 0 else width
    chunks = width // chunk
    head_count = columns // HEAD_DIM
    levels = n // LAYER
    guests = levels - group_levels(levels)
    room = max(guests, 1)
    wings = wings_of(head_count)
    stat_rows = -(-2 * head_count // wings // 8) * 8
    vmem = pltpu.VMEM
    dma = pltpu.SemaphoreType.DMA
    return pl.pallas_call(
        functools.partial(kernel, n, chunk),
        out_shape=jax.ShapeDtypeStruct((half, width), jnp.bfloat16),
        in_specs=[
            pl.BlockSpec(memory_space=pltpu.SMEM),
            pl.BlockSpec(memory_space=pltpu.HBM),
            pl.BlockSpec(memory_space=pltpu.HBM),
            pl.BlockSpec(memory_space=pltpu.HBM),
            pl.BlockSpec(memory_space=pltpu.HBM),
        ],
        out_specs=pl.BlockSpec(memory_space=vmem),
        scratch_shapes=[
            vmem((tok_rows, columns), jnp.bfloat16),
            dma,
            vmem((n * tok_rows, columns), jnp.bfloat16),
            vmem((n * tok_rows, columns), jnp.bfloat16),
            vmem(wo.shape, jnp.bfloat16),
            vmem((head_count, tok_rows, HEAD_DIM), jnp.float32),
            vmem((head_count, tok_rows, 2 * HEAD_DIM), jnp.float32),
            vmem((room * tok_rows, columns), jnp.bfloat16),
            vmem((head_count, room * tok_rows, HEAD_DIM), jnp.float32),
            vmem((head_count, room * tok_rows, 2 * HEAD_DIM), jnp.float32),
            vmem((room, tok_rows, columns), jnp.bfloat16),
            vmem((room, wings, stat_rows, HEAD_DIM), jnp.float32),
            vmem((tok_rows, columns), jnp.bfloat16),
            vmem((wings, stat_rows, HEAD_DIM), jnp.float32),
            vmem((tok_rows, columns), jnp.bfloat16),
            vmem((chunks, half, chunk), jnp.float32),
            vmem((chunks, half, chunk), jnp.bfloat16),
            vmem((chunks, half, chunk), jnp.bfloat16),
            dma((5, 2 * wings, levels)),
            dma((2 * wings, n)),
            dma((2,)),
            dma,
            dma((chunks,)),
            dma((chunks,)),
            dma((wings,)),
            dma((wings, room)),
            dma((2, wings, room)),
            dma((2, wings)),
        ],
        compiler_params=pltpu.CompilerParams(
            collective_id=0, has_side_effects=True, vmem_limit_bytes=52 << 20
        ),
    )(*[pltpu.with_memory_space_constraint(x, pltpu.HBM) for x in (frame_tokens, queries, keys, values, wo)])


def solution(mesh):
    in_specs = (P("ctx", "tp"), P("ctx", "tp"), P("ctx", "tp"), P("tp", None), P())
    out_specs = P(("ctx", "tp"), None)
    return jax.shard_map(
        on_device, mesh=mesh, in_specs=in_specs, out_specs=out_specs, check_vma=False
    )
```
